256 devices in a mesh: gx: 4 (over y), gy: 8 (over x, core), gz: 8 (over z).
Axes of the slice: x: 4, y: 4, z: 8, core: 2. Of those that a mesh axis runs over, the one named last changes fastest.
Arguments:
- data: float32 [128, 256, 1024], P('gx', 'gy', 'gz'), may hold values from -120 to 120
- weights: float32 [8, 1024], P(None, 'gz'), may hold values from -3 to 3
Outputs:
- solution: float32 [128, 256, 1024], P('gx', 'gy', 'gz')
- residual: float32 [128, 256, 1024], P('gx', 'gy', 'gz')
- norms: float32 [4], replicated
The draws below stay inside these ranges and needn't reach their ends.
All inputs are finite; a program needn't handle non-finite values.
Results may differ from the reference program's by a relative error of at most 0.0001.
Values sent between devices are 32-bit elements; how exact they have to be, the bound alone decides.
No kernel may reach another device: no remote copies, remote signals or barrier semaphores. Data moves between devices by JAX's collectives and lax.ppermute only.
A program may use at most 128 MiB of HBM per device.

```python
import math
import jax
import jax.numpy as jnp
from jax import lax

HALF = 4
BAND = 8
NX = 128
NY = 256
NZ = 1024


def draw_data(key, part):
    key_x, key_y, key_z, key_n = jax.random.split(key, 4)
    reach = math.log(10.0) / 3.0
    along_x = jnp.exp(jax.random.uniform(key_x, (NX,), jnp.float32, 0.0, reach)) * 3.0 ** (jnp.arange(NX, dtype=jnp.float32) / NX)
    along_y = jnp.exp(jax.random.uniform(key_y, (NY,), jnp.float32, 0.0, reach)) * 3.0 ** (jnp.arange(NY, dtype=jnp.float32) / NY)
    along_z = jnp.exp(jax.random.uniform(key_z, (NZ,), jnp.float32, 0.0, reach)) * 3.0 ** (jnp.arange(NZ, dtype=jnp.float32) / NZ)
    scales = along_x[:, None, None] * along_y[None, :, None] * along_z[None, None, :] / 15.0
    base = jnp.clip(jax.random.normal(key_n, (NX, NY, NZ), jnp.float32), -6.0, 6.0)
    return (base * scales).astype(jnp.float32)


def block_levels(own_key, dims, cuts, low, top_value):
    factor_of, own = 1.0, jax.random.fold_in(own_key, 6)
    for position, parts in cuts:
        steps = jnp.exp(jax.random.uniform(jax.random.fold_in(own, position), (parts,), jnp.float32, low / len(cuts), top_value / len(cuts)))
        factor_of = factor_of * jnp.repeat(steps, dims[position] // parts).reshape([-1 if axis == position else 1 for axis in range(len(dims))])
    return factor_of


def normal_values(own_key, dims, scale, bound, cuts=(), kind=jnp.bfloat16):
    factor_of = block_levels(own_key, dims, cuts, -0.22, 0.18) if cuts else 1.0
    values = jax.random.normal(own_key, dims, jnp.float32) * scale * factor_of
    return jnp.minimum(jnp.maximum(values, -bound), bound).astype(kind)


def setup_inputs(seed: int = 0) -> dict:
    keys = jax.random.split(jax.random.key(seed), 3)
    return {
        "data": draw_data(jax.random.fold_in(keys[2], 71), 0),
        "weights": normal_values(keys[1], (BAND, NZ), 0.2, 3.0, ((1, 8),), jnp.float32),
    }


relaxation = 0.45

def band_offsets():
    return [j - HALF for j in range(HALF)] + [j - HALF + 1 for j in range(HALF, 2 * HALF)]

def forward_band(padded, weights):
    count = weights.shape[1]
    result = padded[:, :, HALF:HALF + count]
    for j, offset in enumerate(band_offsets()):
        result = result + weights[j][None, None, :] * padded[:, :, HALF + offset:HALF + offset + count]
    return result

def backward_band(padded, transposed):
    count = transposed.shape[1]
    result = padded[:, :, HALF:HALF + count]
    for j, offset in enumerate(band_offsets()):
        result = result + transposed[j][None, None, :] * padded[:, :, HALF - offset:HALF - offset + count]
    return result

def transposed_weights(padded, count):
    return jnp.stack([padded[j, HALF - offset:HALF - offset + count] for j, offset in enumerate(band_offsets())])

def neighbours(padded, width, shape):

    def part(a, b, c):
        return padded[width + a:width + a + shape[0], width + b:width + b + shape[1], width + c:width + c + shape[2]]
    return part(1, 0, 0) + part(-1, 0, 0) + part(0, 1, 0) + part(0, -1, 0) + part(0, 0, 1) + part(0, 0, -1)

def combine(field, back, near, stiffness):
    return back + stiffness * (6.0 * field - near)

def diagonal_of(transposed, stiffness):
    return 1.0 + lax.optimization_barrier(jnp.sum(transposed * transposed, axis=0)) + 6.0 * stiffness

def coarsen(weights):
    return 0.5 * (weights[:, 0::2] + weights[:, 1::2])

def restrict_dim(padded, dim):
    half_count = (padded.shape[dim] - 2) // 2
    s0 = jax.lax.slice_in_dim(padded, 0, 2 * half_count - 1, 2, dim)
    s1 = jax.lax.slice_in_dim(padded, 1, 2 * half_count, 2, dim)
    s2 = jax.lax.slice_in_dim(padded, 2, 2 * half_count + 1, 2, dim)
    s3 = jax.lax.slice_in_dim(padded, 3, 2 * half_count + 2, 2, dim)
    return (s0 + 3.0 * s1 + 3.0 * s2 + s3) * 0.125

def prolong_dim(padded, dim):
    count = padded.shape[dim] - 2
    below = jax.lax.slice_in_dim(padded, 0, count, 1, dim)
    centre = jax.lax.slice_in_dim(padded, 1, count + 1, 1, dim)
    above = jax.lax.slice_in_dim(padded, 2, count + 2, 1, dim)
    even = 0.75 * centre + 0.25 * below
    odd = 0.75 * centre + 0.25 * above
    joined = jnp.stack([even, odd], dim + 1)
    shape = list(centre.shape)
    shape[dim] = 2 * count
    return joined.reshape(shape)

def restrict_all(padded):
    for dim in range(3):
        padded = restrict_dim(padded, dim)
    return padded

def prolong_all(padded):
    for dim in range(3):
        padded = prolong_dim(padded, dim)
    return padded

def zpad(field):
    return jnp.pad(field, ((0, 0), (0, 0), (HALF, HALF)))

def whole_transposed(weights):
    return transposed_weights(jnp.pad(weights, ((0, 0), (HALF, HALF))), weights.shape[1])

def whole_operate(field, weights, transposed, stiffness):
    back = backward_band(zpad(forward_band(zpad(field), weights)), transposed)
    near = neighbours(jnp.pad(field, 1), 1, field.shape)
    return combine(field, back, near, stiffness)

def sweep(error, right, apply_fn, diag):
    return error + relaxation * (right - apply_fn(error)) / diag

def reference(data, weights):
    level_weights = [weights]
    for level in range(3):
        level_weights.append(coarsen(level_weights[-1]))
    level_trans = [whole_transposed(w) for w in level_weights]
    rhs = backward_band(zpad(data), level_trans[0])
    right = rhs
    rights, errors, diags, totals = ([], [], [], [])
    for level in range(3):
        stiffness = 0.25 ** level
        diag = diagonal_of(level_trans[level], stiffness)
        apply_fn = partial_apply(level_weights[level], level_trans[level], stiffness)
        error = relaxation * right / diag
        error = sweep(error, right, apply_fn, diag)
        defect = right - apply_fn(error)
        totals.append(jnp.sum(defect * defect) / defect.size)
        rights.append(right)
        errors.append(error)
        diags.append(diag)
        right = restrict_all(jnp.pad(defect, 1))
    stiffness = 0.25 ** 3
    diag = diagonal_of(level_trans[3], stiffness)
    apply_fn = partial_apply(level_weights[3], level_trans[3], stiffness)
    coarse = relaxation * right / diag
    coarse = sweep(coarse, right, apply_fn, diag)
    for level in (2, 1, 0):
        apply_fn = partial_apply(level_weights[level], level_trans[level], 0.25 ** level)
        update = errors[level] + prolong_all(jnp.pad(coarse, 1))
        update = sweep(update, rights[level], apply_fn, diags[level])
        update = sweep(update, rights[level], apply_fn, diags[level])
        coarse = update
    solution = coarse
    residual = rhs - whole_operate(solution, level_weights[0], level_trans[0], 1.0)
    totals.append(jnp.sum(residual * residual) / residual.size)
    norms = jnp.sqrt(jnp.stack(totals))
    return (solution, residual, norms)

def partial_apply(weights, transposed, stiffness):

    def apply_fn(field):
        return whole_operate(field, weights, transposed, stiffness)
    return apply_fn
```

```python
import jax
import jax.numpy as jnp
from jax import lax
from jax.sharding import PartitionSpec as P
from jax.experimental import pallas as pl
from jax.experimental.pallas import tpu as pltpu

OFFSETS = (-4, -3, -2, -1, 1, 2, 3, 4)
RELAX = 0.45
NX, NY, NZ = 128, 256, 1024
F32, BF16 = jnp.float32, jnp.bfloat16
H0, H1, H2, H3 = 4, 5, 11, 4
S0, S1, S2, S3 = 1.0, 0.25, 0.0625, 0.015625
SLOT = 40
VMEM_LIMIT = 56 * 2**20


def place_0(p):
    return jnp.where(p < 192, p, p - 256)


def place_1(p):
    lane = p & 127
    return jnp.where((lane < 96) == (p < 128), lane, lane - 128)


def place_2(p):
    lane = p & 127
    return jnp.where((lane < 80) == (p < 128), lane, lane - 128)


def place_3(p):
    return jnp.where(p < 64, p, p - 128)


def inside(z, iz, level, reach):
    count = 128 >> level
    glob = iz * count + z
    return (z >= -reach) & (z < count + reach) & (glob >= 0) & (glob < (NZ >> level))


def rows(shape, dim):
    return lax.broadcasted_iota(jnp.int32, shape, dim)


def halves(a):
    hi = a.astype(BF16)
    return hi, (a - hi.astype(F32)).astype(BF16)


def thrice(matrix):
    hi, lo = halves(matrix)
    return jnp.concatenate([hi, hi, lo], axis=0)


def times(field, matrix):
    shape = field.shape
    hi, lo = halves(field.reshape(shape[0] * shape[1], shape[2]))
    out = jnp.dot(jnp.concatenate([hi, lo, hi], axis=1), matrix, preferred_element_type=F32)
    return out.reshape(shape[0], shape[1], matrix.shape[1])


def times_exact(field, matrix):
    shape = field.shape
    hi, lo = halves(field.reshape(shape[0] * shape[1], shape[2]))
    out = jnp.dot(jnp.concatenate([hi, lo], axis=1), matrix, preferred_element_type=F32)
    return out.reshape(shape[0], shape[1], matrix.shape[1])


def operators(w, place, iz, level, reach, stiffness):
    n = w.shape[1]
    zk = place(rows((n, n), 0))
    zn = place(rows((n, n), 1))
    both = inside(zk, iz, level, reach) & inside(zn, iz, level, reach)
    gap = jnp.where(both, zk - zn, 99)
    band = jnp.where(gap == 0, 1.0, 0.0)
    eye = jnp.where(rows((n, n), 0) == rows((n, n), 1), 1.0, 0.0)
    for j, offset in enumerate(OFFSETS):
        band = jnp.where(gap == offset, w[j : j + 1, :], band)
    gram = lax.dot_general(
        band, band, (((1,), (1,)), ((), ())), precision=lax.Precision.HIGHEST, preferred_element_type=F32
    )
    diag = jnp.sum(gram * eye, axis=0, keepdims=True) + 6.0 * stiffness
    line = inside(place(rows((1, n), 1)), iz, level, reach)
    factor = jnp.where(line, RELAX / diag, 0.0)
    op = gram + stiffness * (6.0 * eye - jnp.where((gap == 1) | (gap == -1), 1.0, 0.0))
    return band, op, eye - op * factor, factor


def restrict_matrix(place_f, n_f, place_c, n_c, iz, level, reach):
    zf = place_f(rows((n_f, n_c), 0))
    zc = place_c(rows((n_f, n_c), 1))
    gap = zf - 2 * zc
    near = jnp.where((gap == 0) | (gap == 1), 0.375, 0.0) + jnp.where((gap == -1) | (gap == 2), 0.125, 0.0)
    m = jnp.where(inside(zf, iz, level, reach), near, 0.0).astype(BF16)
    return jnp.concatenate([m, m], axis=0)


def prolong_matrix(place_c, n_c, place_f, n_f, iz, level, reach):
    zc = place_c(rows((n_c, n_f), 0))
    zf = place_f(rows((n_c, n_f), 1))
    gap = zf - 2 * zc
    near = jnp.where((gap == 0) | (gap == 1), 0.75, 0.0) + jnp.where((gap == -1) | (gap == 2), 0.25, 0.0)
    m = jnp.where(inside(zf, iz, level, reach), near, 0.0).astype(BF16)
    return jnp.concatenate([m, m], axis=0)


def plane_mask(shape, level, ix, iy, reach):
    x = ix * (32 >> level) + rows(shape, 0) - reach
    y = iy * (32 >> level) + rows(shape, 1) - reach
    ok = (x >= 0) & (x < (NX >> level)) & (y >= 0) & (y < (NY >> level))
    return jnp.where(ok, 1.0, 0.0)


def around(ref, a, b):
    mid = ref[a:b]
    count = mid.shape[1]
    return mid, (ref[a + 1 : b + 1] + ref[a - 1 : b - 1]) + (pltpu.roll(mid, 1, 1) + pltpu.roll(mid, count - 1, 1))


def chunks(a, b, step):
    return [(c, min(c + step, b)) for c in range(a, b, step)]


def relax(src, dst, a, b, step, matrix, right, side):
    for p, q in chunks(a, b, step):
        mid, near = around(src, p, q)
        dst[p:q] = times(mid, matrix) + right(p, q) + side[p:q] * near


def weights_kernel(pos, w0, w1, b0, k0, m0, f0, k1, m1, f1):
    iz = pos[2]
    band, op, step, factor = operators(w0[...], place_0, iz, 0, 36, S0)
    b0[...] = thrice(jnp.transpose(band))
    k0[...] = thrice(step)
    m0[...] = thrice(op)
    f0[...] = jnp.broadcast_to(factor, (8, 256))
    lane = rows((8, 128), 1)
    first, second = w1[:, :128], w1[:, 128:]
    laid = jnp.concatenate([jnp.where(lane < 96, first, second), jnp.where(lane < 96, second, first)], axis=1)
    band, op, step, factor = operators(laid, place_1, iz, 1, 41, S1)
    k1[...] = thrice(step[:, :128])
    m1[...] = thrice(op[:128, :128])
    f1[...] = jnp.broadcast_to(factor, (8, 256))


def pack_kernel(width, reach, count, n, data, xlo, xhi, ylo, yhi, full, to_left, to_right):
    def plane(p):
        if p >= n + 2 * reach:
            return jnp.zeros(full.shape[1:], F32)
        if p < reach:
            mid = xlo[p]
        elif p < reach + n:
            mid = data[p - reach]
        else:
            mid = xhi[p - reach - n]
        parts = [ylo[p], mid, yhi[p]]
        rest = full.shape[1] - n - 2 * reach
        if rest:
            parts.append(jnp.zeros((rest, count), F32))
        out = jnp.concatenate(parts, axis=0)
        if count < 128:
            out = jnp.concatenate([out, jnp.zeros((full.shape[1], 128 - count), F32)], axis=1)
        return out

    lane = rows(full.shape[1:], 1)
    for g in range(to_left.shape[0]):
        left, right = None, None
        for i in range(3):
            p = 3 * g + i
            value = plane(p)
            if p < full.shape[0]:
                full[p] = value
            a = pltpu.roll(value, SLOT * i, 1) if i else value
            b = pltpu.roll(value, (SLOT * i + width - count) % 128, 1)
            left = a if i == 0 else jnp.where(lane < SLOT * i, left, a)
            right = b if i == 0 else jnp.where(lane < SLOT * i, right, b)
        to_left[g] = left
        to_right[g] = right


def down_0_kernel(pos, dxy, from_right, from_left, b0, k0, m0, f0, r1, e_out, r_out, stat, d, e0, side, g, gx):
    ix, iy, iz = pos[0], pos[1], pos[2]
    lane = rows((40, 128), 1)
    for p in range(40):
        group, i = divmod(p, 3)
        mask = plane_mask((1, 40, 128), 0, ix, iy, H0) if False else None
        xr = ix * 32 + p - H0
        y = iy * 32 + rows((40, 128), 0) - H0
        ok = jnp.where((y >= 0) & (y < NY), jnp.where((xr >= 0) & (xr < NX), 1.0, 0.0), 0.0)
        right = pltpu.roll(from_right[group], (128 - SLOT * i) % 128, 1) if i else from_right[group]
        left = pltpu.roll(from_left[group], (92 - SLOT * i) % 128, 1)
        d[p, :, :128] = dxy[p] * ok
        d[p, :, 128:] = jnp.where(lane < 36, right, jnp.where(lane >= 92, left, 0.0)) * ok
        fs = f0[0:1, :] * S0
        side[p, :, :128] = ok * fs[:, :128]
        side[p, :, 128:] = ok * fs[:, 128:]
    factor = f0[0:1, :].reshape(1, 1, 256)
    for p, q in chunks(0, 40, 8):
        r = times(d[p:q], b0[...])
        r_out[p:q] = r
        e0[p:q] = r * factor
    relax(e0, e_out, 1, 39, 10, k0[...], lambda p, q: e0[p:q], side)
    e_out[0] = jnp.zeros((40, 256), F32)
    e_out[39] = jnp.zeros((40, 256), F32)
    total = jnp.zeros((40, 128), F32)
    for p, q in chunks(3, 37, 9):
        mid, near = around(e_out, p, q)
        value = r_out[p:q] - times(mid, m0[...]) + S0 * near
        x = ix * 32 + rows(value.shape, 0) + (p - H0)
        y = iy * 32 + rows(value.shape, 1) - H0
        value = jnp.where((x >= 0) & (x < NX) & (y >= 0) & (y < NY), value, 0.0)
        g[p:q] = value
        own = value[max(p, 4) - p : min(q, 36) - p, :, :128]
        total = total + jnp.sum(own * own, axis=0)
    row = rows((40, 128), 0)
    stat[...] = jnp.full((8, 128), jnp.sum(jnp.where((row >= 4) & (row < 36), total, 0.0)), F32)
    for i in range(16):
        value = ((g[2 * i + 3] + g[2 * i + 6]) + 3.0 * (g[2 * i + 4] + g[2 * i + 5])) * 0.125
        gx[i, 0] = value[:, :128]
        gx[i, 1] = value[:, 128:]
    gy = [
        jnp.concatenate([gx[:, t, pl.ds(3 + a, 16, stride=2), :] for t in range(2)], axis=2) for a in range(4)
    ]
    gy = ((gy[0] + gy[3]) + 3.0 * (gy[1] + gy[2])) * 0.125
    fold = restrict_matrix(place_0, 256, lambda q: q, 128, iz, 0, 36)
    r1[...] = times_exact(gy, fold)[:, :, :64]


def down_1_kernel(pos, rxy, from_right, from_left, k1, m1, f1, w2, msg, e_out, r_out, stat, e0, e0b, side, g, gx):
    ix, iy, iz = pos[0], pos[1], pos[2]
    lane = rows((32, 128), 1)
    for p in range(26):
        group, i = divmod(p, 3)
        xr = ix * 16 + p - H1
        yrow = rows((32, 128), 0)
        y = iy * 16 + yrow - H1
        ok = jnp.where(
            (y >= 0) & (y < NY // 2) & (yrow < 26), jnp.where((xr >= 0) & (xr < NX // 2), 1.0, 0.0), 0.0
        )
        right = pltpu.roll(from_right[group], (64 - SLOT * i) % 128, 1)
        left = pltpu.roll(from_left[group], (91 - SLOT * i) % 128, 1)
        first = jnp.where(lane < 64, rxy[p], jnp.where(lane < 101, right, 0.0))
        second = jnp.where(lane >= 91, left, 0.0)
        main = jnp.where(lane < 96, first, second) * ok
        rest = jnp.where(lane < 96, second, first) * ok
        r_out[p] = main
        e0[p] = main * f1[0:1, :128]
        e0b[p] = rest * f1[0:1, 128:]
        side[p] = ok * (f1[0:1, :128] * S1)
    for p, q in chunks(1, 25, 8):
        mid, near = around(e0, p, q)
        both = jnp.concatenate([mid, e0b[p:q]], axis=2)
        e_out[p:q] = times(both, k1[...]) + mid + side[p:q] * near
    e_out[0] = jnp.zeros((32, 128), F32)
    e_out[25] = jnp.zeros((32, 128), F32)
    total = jnp.zeros((32, 128), F32)
    for p, q in chunks(4, 22, 9):
        mid, near = around(e_out, p, q)
        value = r_out[p:q] - times(mid, m1[...]) + S1 * near
        x = ix * 16 + rows(value.shape, 0) + (p - H1)
        y = iy * 16 + rows(value.shape, 1) - H1
        value = jnp.where((x >= 0) & (x < NX // 2) & (y >= 0) & (y < NY // 2), value, 0.0)
        g[p:q] = value
        own = value[max(p, 5) - p : min(q, 21) - p]
        total = total + jnp.sum(own * own, axis=0)
    row = rows((32, 128), 0)
    keep = (row >= 5) & (row < 21) & (lane < 64)
    stat[...] = jnp.full((8, 128), jnp.sum(jnp.where(keep, total, 0.0)), F32)
    for i in range(8):
        gx[i] = ((g[2 * i + 4] + g[2 * i + 7]) + 3.0 * (g[2 * i + 5] + g[2 * i + 6])) * 0.125
    gy = [gx[:, pl.ds(4 + a, 8, stride=2), :] for a in range(4)]
    gy = ((gy[0] + gy[3]) + 3.0 * (gy[1] + gy[2])) * 0.125
    fold = restrict_matrix(place_1, 128, lambda q: q, 128, iz, 1, 32)
    msg[:8] = times_exact(gy, fold)[:, :, :32]
    msg[8] = w2[...]


def weights_2_kernel(pos, w2, w3, k2, k2u, m2, f2, k3, f3):
    iz = pos[2]
    lane = rows((8, 128), 1)
    first, second = w2[:, :128], w2[:, 128:]
    laid = jnp.concatenate([jnp.where(lane < 80, first, second), jnp.where(lane < 80, second, first)], axis=1)
    band, op, step, factor = operators(laid, place_2, iz, 2, 69, S2)
    k2[...] = thrice(step)
    k2u[...] = thrice(step[:128, :128])
    m2[...] = thrice(op)
    f2[...] = jnp.broadcast_to(factor, (8, 256))
    band, op, step, factor = operators(w3[...], place_3, iz, 3, 28, S3)
    k3[...] = thrice(step)
    f3[...] = jnp.broadcast_to(factor, (8, 128))


def up_kernel(
    pos, r2x, ya, yb, yc, yd, k2, k2u, m2, f2, k3, f3,
    k1, f1, e1s, r1s, k0, m0, f0, e0s, r0s, stat0, stat1,
    sol, res, stat,
    ra, ea, eb, side2, gx2, r3, e3, side3, c3, cy2, ua, ub, side1, cy1, va, vb, side0, cy0,
):
    ix, iy, iz = pos[0], pos[1], pos[2]
    lane = rows((32, 128), 1)
    yrow = rows((32, 128), 0)
    for p in range(30):
        xr = ix * 8 + p - H2
        y = iy * 8 + yrow - H2
        ok = jnp.where(
            (y >= 0) & (y < NY // 4) & (yrow < 30), jnp.where((xr >= 0) & (xr < NX // 4), 1.0, 0.0), 0.0
        )
        full = jnp.concatenate([yc[p], ya[p], r2x[p], yb[p], yd[p], jnp.zeros((2, 256), F32)], axis=0)
        first, second = full[:, :128], full[:, 128:]
        main = jnp.where(lane < 80, first, second) * ok
        rest = jnp.where(lane < 80, second, first) * ok
        ra[p, :, :128] = main
        ra[p, :, 128:] = rest
        ea[p, :, :128] = main * f2[0:1, :128]
        ea[p, :, 128:] = rest * f2[0:1, 128:]
        side2[p, :, :128] = ok * (f2[0:1, :128] * S2)
        side2[p, :, 128:] = ok * (f2[0:1, 128:] * S2)
    relax(ea, eb, 1, 29, 10, k2[...], lambda p, q: ea[p:q], side2)
    total = jnp.zeros((32, 128), F32)
    for p, q in chunks(2, 28, 13):
        mid, near = around(eb, p, q)
        value = ra[p:q] - times(mid, m2[...]) + S2 * near
        x = ix * 8 + rows(value.shape, 0) + (p - H2)
        y = iy * 8 + rows(value.shape, 1) - H2
        value = jnp.where((x >= 0) & (x < NX // 4) & (y >= 0) & (y < NY // 4), value, 0.0)
        ea[p:q] = value
        own = value[max(p, 11) - p : min(q, 19) - p, :, :128]
        total = total + jnp.sum(own * own, axis=0)
    keep = (yrow >= 11) & (yrow < 19) & (lane < 32)
    sum2 = jnp.sum(jnp.where(keep, total, 0.0))
    for i in range(12):
        value = ((ea[2 * i + 2] + ea[2 * i + 5]) + 3.0 * (ea[2 * i + 3] + ea[2 * i + 4])) * 0.125
        gx2[i, 0, :32] = value[:, :128]
        gx2[i, 1, :32] = value[:, 128:]
        gx2[i, 0, 32:] = jnp.zeros((8, 128), F32)
        gx2[i, 1, 32:] = jnp.zeros((8, 128), F32)
    gy = [
        jnp.concatenate([gx2[:, t, pl.ds(2 + a, 16, stride=2), :] for t in range(2)], axis=2) for a in range(4)
    ]
    gy = ((gy[0] + gy[3]) + 3.0 * (gy[1] + gy[2])) * 0.125
    fold = restrict_matrix(place_2, 256, place_3, 128, iz, 2, 65)
    mask = plane_mask((12, 16, 128), 3, ix, iy, H3)
    right3 = times_exact(gy, fold) * mask
    factor3 = f3[0:1, :].reshape(1, 1, 128)
    e3[...] = right3 * factor3
    side3[...] = mask * (factor3 * S3)
    c3[...] = jnp.zeros((12, 16, 128), F32)
    relax(e3, c3, 1, 11, 10, k3[...], lambda p, q: e3[p:q], side3)
    grow = prolong_matrix(place_3, 128, place_2, 128, iz, 2, 69)
    cz = times_exact(c3[...], grow)
    below, above = pltpu.roll(cz, 1, 1), pltpu.roll(cz, 15, 1)
    cy2[...] = jnp.zeros((12, 32, 128), F32)
    cy2[:, pl.ds(3, 12, stride=2), :] = (0.75 * cz + 0.25 * below)[:, :12]
    cy2[:, pl.ds(4, 12, stride=2), :] = (0.75 * cz + 0.25 * above)[:, :12]
    ua2, ub2 = r3, gx2
    fr2 = f2[0:1, :128].reshape(1, 1, 128)
    for xf in range(6, 24):
        f = xf - H2
        j = f // 2 + 4
        other = j - 1 if f % 2 == 0 else j + 1
        xr = ix * 8 + f
        y = iy * 8 + yrow - H2
        ok = jnp.where((y >= 0) & (y < NY // 4), jnp.where((xr >= 0) & (xr < NX // 4), 1.0, 0.0), 0.0)
        ea[xf, :, :128] = eb[xf, :, :128] + ok * (0.75 * cy2[j] + 0.25 * cy2[other])

    def relax_2(src, dst, a, b):
        for p, q in chunks(a, b, 8):
            mid = src[p:q, :, :128]
            near = (src[p + 1 : q + 1, :, :128] + src[p - 1 : q - 1, :, :128]) + (
                pltpu.roll(mid, 1, 1) + pltpu.roll(mid, 31, 1)
            )
            dst[p:q, :, :128] = times(mid, k2u[...]) + fr2 * ra[p:q, :, :128] + side2[p:q, :, :128] * near

    relax_2(ea, eb, 7, 23)
    relax_2(eb, ea, 8, 22)
    grow = prolong_matrix(place_2, 128, place_1, 128, iz, 1, 41)
    for p in range(14):
        r3[p] = ea[8 + p, :, :128]
    r3[...] = times_exact(r3[...], grow)
    cy1[...] = jnp.zeros((14, 32, 128), F32)
    cy1[:, pl.ds(1, 12, stride=2), :] = 0.75 * r3[:, 9:21, :] + 0.25 * r3[:, 8:20, :]
    cy1[:, pl.ds(2, 12, stride=2), :] = 0.75 * r3[:, 9:21, :] + 0.25 * r3[:, 10:22, :]
    fr1 = f1[0:1, :128].reshape(1, 1, 128)
    for xf in range(26):
        f = xf - H1
        xr = ix * 16 + f
        y = iy * 16 + yrow - H1
        ok = jnp.where((y >= 0) & (y < NY // 2), jnp.where((xr >= 0) & (xr < NX // 2), 1.0, 0.0), 0.0)
        side1[xf] = ok * (f1[0:1, :128] * S1)
        if 1 <= xf <= 24:
            j = f // 2 + 3
            other = j - 1 if f % 2 == 0 else j + 1
            ua[xf] = e1s[xf] + ok * (0.75 * cy1[j] + 0.25 * cy1[other])
    relax(ua, ub, 2, 24, 11, k1[...], lambda p, q: fr1 * r1s[p:q], side1)
    relax(ub, ua, 3, 23, 10, k1[...], lambda p, q: fr1 * r1s[p:q], side1)
    grow = prolong_matrix(place_1, 128, place_0, 256, iz, 0, 36)
    for p, q in chunks(0, 20, 10):
        cz = times_exact(ua[3 + p : 3 + q], grow)
        for t in range(2):
            part = cz[:, :, 128 * t : 128 * t + 128]
            cy0[p:q, t, pl.ds(0, 20, stride=2), :] = 0.75 * part[:, 3:23] + 0.25 * part[:, 2:22]
            cy0[p:q, t, pl.ds(1, 20, stride=2), :] = 0.75 * part[:, 3:23] + 0.25 * part[:, 4:24]
    fr0 = f0[0:1, :].reshape(1, 1, 256)
    for xf in range(40):
        f = xf - H0
        xr = ix * 32 + f
        y = iy * 32 + rows((40, 128), 0) - H0
        ok = jnp.where((y >= 0) & (y < NY), jnp.where((xr >= 0) & (xr < NX), 1.0, 0.0), 0.0)
        for t in range(2):
            part = slice(128 * t, 128 * t + 128)
            side0[xf, :, part] = ok * (f0[0:1, part] * S0)
            if 1 <= xf <= 38:
                j = f // 2 + 2
                other = j - 1 if f % 2 == 0 else j + 1
                va[xf, :, part] = e0s[xf, :, part] + ok * (0.75 * cy0[j, t] + 0.25 * cy0[other, t])
    relax(va, vb, 2, 38, 9, k0[...], lambda p, q: fr0 * r0s[p:q], side0)
    relax(vb, va, 3, 37, 9, k0[...], lambda p, q: fr0 * r0s[p:q], side0)
    total = jnp.zeros((32, 128), F32)
    last = m0[:, :128]
    for p, q in chunks(4, 36, 8):
        mid = va[p:q]
        flat = va[p:q, :, :128]
        near = (va[p + 1 : q + 1, :, :128] + va[p - 1 : q - 1, :, :128]) + (
            pltpu.roll(flat, 1, 1) + pltpu.roll(flat, 39, 1)
        )
        value = (r0s[p:q, :, :128] - times(mid, last) + S0 * near)[:, 4:36]
        res[p - 4 : q - 4] = value
        sol[p - 4 : q - 4] = va[p:q, 4:36, :128]
        total = total + jnp.sum(value * value, axis=0)
    sum3 = jnp.sum(total)
    tile = rows((8, 128), 1)
    stat[...] = jnp.where(
        tile == 0, stat0[...], jnp.where(tile == 1, stat1[...], jnp.where(tile == 2, sum2, jnp.where(tile == 3, sum3, 0.0)))
    )


def shift(x, axis, k):
    n = lax.axis_size(axis)
    return lax.ppermute(x, axis, [((i + k) % n, i) for i in range(n)])


def swap(x, axes, sizes, flip):
    n = 1
    for s in sizes:
        n *= s
    return lax.ppermute(x, axes, [(i ^ flip, i) for i in range(n)])


def f32(*shape):
    return jax.ShapeDtypeStruct(shape, F32)


def bf16(*shape):
    return jax.ShapeDtypeStruct(shape, BF16)


def scratch(*shape):
    return pltpu.VMEM(shape, F32)


def call(kernel, outs, scratches, n_in, name, scalars=True):
    specs = [pl.BlockSpec(memory_space=pltpu.SMEM)] if scalars else []
    specs += [pl.BlockSpec(memory_space=pltpu.VMEM)] * n_in
    return pl.pallas_call(
        kernel,
        out_shape=outs,
        in_specs=specs,
        out_specs=[pl.BlockSpec(memory_space=pltpu.VMEM)] * len(outs),
        scratch_shapes=scratches,
        compiler_params=pltpu.CompilerParams(vmem_limit_bytes=VMEM_LIMIT),
        name=name,
    )


def coarsen(w):
    return 0.5 * (w[:, 0::2] + w[:, 1::2])


def pack(width, reach, count, n, height, groups, parts, name):
    def kernel(*refs):
        pack_kernel(width, reach, count, n, *refs)

    outs = [f32(n + 2 * reach, height, 128), f32(groups, height, 128), f32(groups, height, 128)]
    return call(kernel, outs, [], 5, name, scalars=False)(*parts)


def sides(block, reach):
    n = block.shape[0]
    xlo = shift(block[n - reach :], "gx", -1)
    xhi = shift(block[:reach], "gx", 1)
    top = jnp.concatenate([xlo[:, n - reach :], block[:, n - reach :], xhi[:, n - reach :]], axis=0)
    bottom = jnp.concatenate([xlo[:, :reach], block[:, :reach], xhi[:, :reach]], axis=0)
    return block, xlo, xhi, shift(top, "gy", -1), shift(bottom, "gy", 1)


def body(data, weights):
    pos = jnp.stack([lax.axis_index("gx"), lax.axis_index("gy"), lax.axis_index("gz")]).astype(jnp.int32)
    w1 = coarsen(weights)
    w2 = coarsen(w1)
    both = jnp.concatenate([weights, w1], axis=1)
    wl, wr = shift(both, "gz", -1), shift(both, "gz", 1)
    wide0 = jnp.concatenate([weights, wr[:, :64], wl[:, 64:128]], axis=1)
    wide1 = jnp.concatenate([w1, wr[:, 128:], wl[:, 128:], wl[:, 128:]], axis=1)
    b0, k0, m0, f0, k1, m1, f1 = call(
        weights_kernel,
        [bf16(768, 256), bf16(768, 256), bf16(768, 256), f32(8, 256), bf16(768, 128), bf16(384, 128), f32(8, 256)],
        [], 2, "weights_fine",
    )(pos, wide0, wide1)
    dxy, to_left, to_right = pack(36, H0, 128, 32, 40, 14, sides(data, H0), "pack_data")
    from_right, from_left = shift(to_left, "gz", 1), shift(to_right, "gz", -1)
    big = (40, 40, 256)
    r1, e0s, r0s, stat0 = call(
        down_0_kernel,
        [f32(16, 16, 64), f32(*big), f32(*big), f32(8, 128)],
        [scratch(*big), scratch(*big), scratch(*big), scratch(*big), scratch(16, 2, 40, 128)],
        7, "down_0",
    )(pos, dxy, from_right, from_left, b0, k0, m0, f0)
    rxy, to_left, to_right = pack(37, H1, 64, 16, 32, 9, sides(r1, H1), "pack_r1")
    from_right, from_left = shift(to_left, "gz", 1), shift(to_right, "gz", -1)
    mid = (26, 32, 128)
    msg, e1s, r1s, stat1 = call(
        down_1_kernel,
        [f32(9, 8, 32), f32(*mid), f32(*mid), f32(8, 128)],
        [scratch(*mid), scratch(*mid), scratch(*mid), scratch(*mid), scratch(8, 32, 128)],
        7, "down_1",
    )(pos, rxy, from_right, from_left, k1, m1, f1, w2)
    near = {k: shift(msg, "gz", k) for k in (1, -1, 2, -2, 3, -3)}
    wide = jnp.concatenate([msg, near[1], near[2], near[3], jnp.zeros_like(msg), near[-3], near[-2], near[-1]], axis=2)
    wide2 = wide[8]
    k2, k2u, m2, f2, k3, f3 = call(
        weights_2_kernel,
        [bf16(768, 256), bf16(384, 128), bf16(768, 256), f32(8, 256), bf16(384, 128), f32(8, 128)],
        [], 2, "weights_coarse",
    )(pos, wide2, coarsen(wide2))
    r2z = wide[:8]
    x1, x2, x3 = (shift(r2z, "gx", k) for k in (1, 2, 3))
    r2x = jnp.concatenate([x2[5:], x3, r2z, x1, x2[:3]], axis=0)
    ya, yb = shift(r2x, "gy", -1), shift(r2x, "gy", 1)
    yc, yd = shift(r2x[:, 5:], "gy", -2), shift(r2x[:, :3], "gy", 2)
    k1u = jnp.concatenate([k1[:128], k1[256:384], k1[512:640]], axis=0)
    lev2 = (30, 32, 256)
    sol, res, stat = call(
        up_kernel,
        [f32(32, 32, 128), f32(32, 32, 128), f32(8, 128)],
        [
            scratch(*lev2), scratch(*lev2), scratch(*lev2), scratch(*lev2), scratch(12, 2, 40, 128),
            scratch(14, 32, 128), scratch(12, 16, 128), scratch(12, 16, 128), scratch(12, 16, 128),
            scratch(12, 32, 128), scratch(*mid), scratch(*mid), scratch(*mid), scratch(14, 32, 128),
            scratch(*big), scratch(*big), scratch(*big), scratch(20, 2, 40, 128),
        ],
        22, "up",
    )(pos, r2x, ya, yb, yc, yd, k2, k2u, m2, f2, k3, f3, k1u, f1, e1s, r1s, k0, m0, f0, e0s, r0s, stat0, stat1)
    t = stat[:1]
    for axes, sizes, flips in (
        ("gx", (4,), (1, 2, 3)),
        ("gy", (8,), (2, 4, 6)),
        (("gy", "gz"), (8, 8), (1, 8, 9)),
        ("gz", (8,), (2, 4, 6)),
    ):
        a, b, c = (swap(t, axes, sizes, f) for f in flips)
        t = (t + a) + (b + c)
    cells = jnp.array([NX * NY * NZ >> (3 * k) for k in (0, 1, 2, 0)], F32)
    return sol, res, jnp.sqrt(t[0, :4] / cells)


def solution(mesh):
    placed = (P("gx", "gy", "gz"), P(None, "gz"))
    return jax.shard_map(
        body,
        mesh=mesh,
        in_specs=placed,
        out_specs=(P("gx", "gy", "gz"), P("gx", "gy", "gz"), P()),
        check_vma=False,
    )
```

```python
import jax
import jax.numpy as jnp
from jax import lax
from jax.sharding import PartitionSpec as P
from jax.experimental import pallas as pl
from jax.experimental.pallas import tpu as pltpu

OFFSETS = (-4, -3, -2, -1, 1, 2, 3, 4)
RELAX = 0.45
NX, NY, NZ = 128, 256, 1024
F32, BF16 = jnp.float32, jnp.bfloat16
H0, H1, H2, H3 = 4, 5, 11, 4
S0, S1, S2, S3 = 1.0, 0.25, 0.0625, 0.015625
SLOT = 40


def place_0(p):
    return jnp.where(p < 192, p, p - 256)


def place_1(p):
    lane = p & 127
    return jnp.where((lane < 96) == (p < 128), lane, lane - 128)


def place_2(p):
    lane = p & 127
    return jnp.where((lane < 80) == (p < 128), lane, lane - 128)


def place_3(p):
    return jnp.where(p < 64, p, p - 128)


def inside(z, iz, level, reach):
    count = 128 >> level
    glob = iz * count + z
    return (z >= -reach) & (z < count + reach) & (glob >= 0) & (glob < (NZ >> level))


def rows(shape, dim):
    return lax.broadcasted_iota(jnp.int32, shape, dim)


def halves(a):
    hi = a.astype(BF16)
    return hi, (a - hi.astype(F32)).astype(BF16)


def thrice(matrix):
    hi, lo = halves(matrix)
    return jnp.concatenate([hi, hi, lo], axis=0)


def times(field, matrix):
    shape = field.shape
    hi, lo = halves(field.reshape(shape[0] * shape[1], shape[2]))
    out = jnp.dot(jnp.concatenate([hi, lo, hi], axis=1), matrix, preferred_element_type=F32)
    return out.reshape(shape[0], shape[1], matrix.shape[1])


def times_exact(field, matrix):
    shape = field.shape
    hi, lo = halves(field.reshape(shape[0] * shape[1], shape[2]))
    out = jnp.dot(jnp.concatenate([hi, lo], axis=1), matrix, preferred_element_type=F32)
    return out.reshape(shape[0], shape[1], matrix.shape[1])


def exact(a, b):
    return jnp.dot(a, b, precision=lax.Precision.HIGHEST, preferred_element_type=F32)


def operators(w, place, iz, level, reach, stiffness):
    n = w.shape[1]
    zk = place(rows((n, n), 0))
    zn = place(rows((n, n), 1))
    both = inside(zk, iz, level, reach) & inside(zn, iz, level, reach)
    gap = jnp.where(both, zk - zn, 99)
    band = jnp.where(gap == 0, 1.0, 0.0)
    eye = jnp.where(rows((n, n), 0) == rows((n, n), 1), 1.0, 0.0)
    for j, offset in enumerate(OFFSETS):
        band = jnp.where(gap == offset, w[j : j + 1, :], band)
    gram = lax.dot_general(
        band, band, (((1,), (1,)), ((), ())), precision=lax.Precision.HIGHEST, preferred_element_type=F32
    )
    diag = jnp.sum(gram * eye, axis=0, keepdims=True) + 6.0 * stiffness
    line = inside(place(rows((1, n), 1)), iz, level, reach)
    factor = jnp.where(line, RELAX / diag, 0.0)
    op = gram + stiffness * (6.0 * eye - jnp.where((gap == 1) | (gap == -1), 1.0, 0.0))
    return band, op, eye - op * factor, factor


def restrict_matrix(place_f, n_f, place_c, n_c, iz, level, reach):
    zf = place_f(rows((n_f, n_c), 0))
    zc = place_c(rows((n_f, n_c), 1))
    gap = zf - 2 * zc
    near = jnp.where((gap == 0) | (gap == 1), 0.375, 0.0) + jnp.where((gap == -1) | (gap == 2), 0.125, 0.0)
    m = jnp.where(inside(zf, iz, level, reach), near, 0.0).astype(BF16)
    return jnp.concatenate([m, m], axis=0)


def prolong_matrix(place_c, n_c, place_f, n_f, iz, level, reach):
    zc = place_c(rows((n_c, n_f), 0))
    zf = place_f(rows((n_c, n_f), 1))
    gap = zf - 2 * zc
    near = jnp.where((gap == 0) | (gap == 1), 0.75, 0.0) + jnp.where((gap == -1) | (gap == 2), 0.25, 0.0)
    m = jnp.where(inside(zf, iz, level, reach), near, 0.0).astype(BF16)
    return jnp.concatenate([m, m], axis=0)


def plane_mask(shape, level, ix, iy, reach):
    x = ix * (32 >> level) + rows(shape, 0) - reach
    y = iy * (32 >> level) + rows(shape, 1) - reach
    ok = (x >= 0) & (x < (NX >> level)) & (y >= 0) & (y < (NY >> level))
    return jnp.where(ok, 1.0, 0.0)


def around(ref, a, b):
    mid = ref[a:b]
    count = mid.shape[1]
    return mid, (ref[a + 1 : b + 1] + ref[a - 1 : b - 1]) + (pltpu.roll(mid, 1, 1) + pltpu.roll(mid, count - 1, 1))


def chunks(a, b, step):
    return [(c, min(c + step, b)) for c in range(a, b, step)]


def relax(src, dst, a, b, step, matrix, right, side):
    for p, q in chunks(a, b, step):
        mid, near = around(src, p, q)
        dst[p:q] = times(mid, matrix) + right(p, q) + side[p:q] * near


def prepare_kernel(data, own, first, last, low, high):
    own[...] = data[...]
    first[...] = data[:H0]
    last[...] = data[32 - H0 :]
    low[...] = data[:, :H0]
    high[...] = data[:, 32 - H0 :]


def weights_0_kernel(left, own, right, b0, k0, m0, f0):
    iz = lax.axis_index("gz")
    lane = rows((8, 128), 1)
    laid = jnp.concatenate([own[...], jnp.where(lane < 64, right[14, :8], left[14, :8])], axis=1)
    band, op, step, factor = operators(laid, place_0, iz, 0, 36, S0)
    b0[...] = thrice(jnp.transpose(band))
    k0[...] = thrice(step)
    m0[...] = thrice(op)
    f0[...] = jnp.broadcast_to(factor, (8, 256))


def weights_1_kernel(left, own, right, k1, k1u, m1, f1):
    iz = lax.axis_index("gz")
    wide = jnp.concatenate([left[14, :8], own[...], right[14, :8]], axis=1)
    mean = jnp.where((rows((384, 256), 0) - 128) >> 1 == place_1(rows((384, 256), 1)), 0.5, 0.0)
    band, op, step, factor = operators(exact(wide, mean), place_1, iz, 1, 41, S1)
    k1[...] = thrice(step[:, :128])
    k1u[...] = thrice(step[:128, :128])
    m1[...] = thrice(op[:128, :128])
    f1[...] = jnp.broadcast_to(factor, (8, 256))


def pack_kernel(width, reach, count, n, data, xlo, xhi, ylo, yhi, extra, full, to_left, to_right):
    def plane(p):
        if p >= n + 2 * reach:
            return jnp.zeros(full.shape[1:], F32)
        if p < reach:
            mid = xlo[p]
        elif p < reach + n:
            mid = data[p - reach]
        else:
            mid = xhi[p - reach - n]
        parts = [ylo[p], mid, yhi[p]]
        rest = full.shape[1] - n - 2 * reach
        if rest:
            parts.append(jnp.zeros((rest, count), F32))
        out = jnp.concatenate(parts, axis=0)
        if count < 128:
            out = jnp.concatenate([out, jnp.zeros((full.shape[1], 128 - count), F32)], axis=1)
        return out

    lane = rows(full.shape[1:], 1)
    groups = to_left.shape[0]
    if extra is not None:
        groups -= 1
        for out in (to_left, to_right):
            out[groups] = jnp.zeros(full.shape[1:], F32)
            out[groups, :8] = extra[...]
    for g in range(groups):
        left, right = None, None
        for i in range(3):
            p = 3 * g + i
            value = plane(p)
            if p < full.shape[0]:
                full[p] = value
            a = pltpu.roll(value, SLOT * i, 1) if i else value
            b = pltpu.roll(value, (SLOT * i + width - count) % 128, 1)
            left = a if i == 0 else jnp.where(lane < SLOT * i, left, a)
            right = b if i == 0 else jnp.where(lane < SLOT * i, right, b)
        to_left[g] = left
        to_right[g] = right


def down_0_kernel(dxy, from_right, from_left, b0, k0, m0, f0, r1, r1_top, r1_bottom, e_out, r_out, stat, d, e0, side, g, gx):
    ix, iy, iz = lax.axis_index("gx"), lax.axis_index("gy"), lax.axis_index("gz")
    lane = rows((40, 128), 1)
    for p in range(40):
        group, i = divmod(p, 3)
        xr = ix * 32 + p - H0
        y = iy * 32 + rows((40, 128), 0) - H0
        ok = jnp.where((y >= 0) & (y < NY), jnp.where((xr >= 0) & (xr < NX), 1.0, 0.0), 0.0)
        right = pltpu.roll(from_right[group], (128 - SLOT * i) % 128, 1) if i else from_right[group]
        left = pltpu.roll(from_left[group], (92 - SLOT * i) % 128, 1)
        d[p, :, :128] = dxy[p] * ok
        d[p, :, 128:] = jnp.where(lane < 36, right, jnp.where(lane >= 92, left, 0.0)) * ok
        fs = f0[0:1, :] * S0
        side[p, :, :128] = ok * fs[:, :128]
        side[p, :, 128:] = ok * fs[:, 128:]
    factor = f0[0:1, :].reshape(1, 1, 256)
    for p, q in chunks(0, 40, 8):
        r = times(d[p:q], b0[...])
        r_out[p:q] = r
        e0[p:q] = r * factor
    relax(e0, e_out, 1, 39, 10, k0[...], lambda p, q: e0[p:q], side)
    e_out[0] = jnp.zeros((40, 256), F32)
    e_out[39] = jnp.zeros((40, 256), F32)
    total = jnp.zeros((40, 128), F32)
    for p, q in chunks(3, 37, 9):
        mid, near = around(e_out, p, q)
        value = r_out[p:q] - times(mid, m0[...]) + S0 * near
        x = ix * 32 + rows(value.shape, 0) + (p - H0)
        y = iy * 32 + rows(value.shape, 1) - H0
        value = jnp.where((x >= 0) & (x < NX) & (y >= 0) & (y < NY), value, 0.0)
        g[p:q] = value
        own = value[max(p, 4) - p : min(q, 36) - p, :, :128]
        total = total + jnp.sum(own * own, axis=0)
    row = rows((40, 128), 0)
    stat[...] = jnp.full((8, 128), jnp.sum(jnp.where((row >= 4) & (row < 36), total, 0.0)), F32)
    for i in range(16):
        value = ((g[2 * i + 3] + g[2 * i + 6]) + 3.0 * (g[2 * i + 4] + g[2 * i + 5])) * 0.125
        gx[i, 0] = value[:, :128]
        gx[i, 1] = value[:, 128:]
    gy = [
        jnp.concatenate([gx[:, t, pl.ds(3 + a, 16, stride=2), :] for t in range(2)], axis=2) for a in range(4)
    ]
    gy = ((gy[0] + gy[3]) + 3.0 * (gy[1] + gy[2])) * 0.125
    fold = restrict_matrix(place_0, 256, lambda q: q, 128, iz, 0, 36)
    out = times_exact(gy, fold)[:, :, :64]
    r1[...] = out
    r1_top[...] = out[:, 16 - H1 :]
    r1_bottom[...] = out[:, :H1]


def down_1_kernel(rxy, from_right, from_left, k1, m1, f1, w, msg, e_out, r_out, stat, e0, e0b, side, g, gx):
    ix, iy, iz = lax.axis_index("gx"), lax.axis_index("gy"), lax.axis_index("gz")
    lane = rows((32, 128), 1)
    for p in range(26):
        group, i = divmod(p, 3)
        xr = ix * 16 + p - H1
        yrow = rows((32, 128), 0)
        y = iy * 16 + yrow - H1
        ok = jnp.where(
            (y >= 0) & (y < NY // 2) & (yrow < 26), jnp.where((xr >= 0) & (xr < NX // 2), 1.0, 0.0), 0.0
        )
        right = pltpu.roll(from_right[group], (64 - SLOT * i) % 128, 1)
        left = pltpu.roll(from_left[group], (91 - SLOT * i) % 128, 1)
        first = jnp.where(lane < 64, rxy[p], jnp.where(lane < 101, right, 0.0))
        second = jnp.where(lane >= 91, left, 0.0)
        main = jnp.where(lane < 96, first, second) * ok
        rest = jnp.where(lane < 96, second, first) * ok
        r_out[p] = main
        e0[p] = main * f1[0:1, :128]
        e0b[p] = rest * f1[0:1, 128:]
        side[p] = ok * (f1[0:1, :128] * S1)
    for p, q in chunks(1, 25, 8):
        mid, near = around(e0, p, q)
        both = jnp.concatenate([mid, e0b[p:q]], axis=2)
        e_out[p:q] = times(both, k1[...]) + mid + side[p:q] * near
    e_out[0] = jnp.zeros((32, 128), F32)
    e_out[25] = jnp.zeros((32, 128), F32)
    total = jnp.zeros((32, 128), F32)
    for p, q in chunks(4, 22, 9):
        mid, near = around(e_out, p, q)
        value = r_out[p:q] - times(mid, m1[...]) + S1 * near
        x = ix * 16 + rows(value.shape, 0) + (p - H1)
        y = iy * 16 + rows(value.shape, 1) - H1
        value = jnp.where((x >= 0) & (x < NX // 2) & (y >= 0) & (y < NY // 2), value, 0.0)
        g[p:q] = value
        own = value[max(p, 5) - p : min(q, 21) - p]
        total = total + jnp.sum(own * own, axis=0)
    row = rows((32, 128), 0)
    keep = (row >= 5) & (row < 21) & (lane < 64)
    stat[...] = jnp.full((8, 128), jnp.sum(jnp.where(keep, total, 0.0)), F32)
    for i in range(8):
        gx[i] = ((g[2 * i + 4] + g[2 * i + 7]) + 3.0 * (g[2 * i + 5] + g[2 * i + 6])) * 0.125
    gy = [gx[:, pl.ds(4 + a, 8, stride=2), :] for a in range(4)]
    gy = ((gy[0] + gy[3]) + 3.0 * (gy[1] + gy[2])) * 0.125
    fold = restrict_matrix(place_1, 128, lambda q: q, 128, iz, 1, 32)
    msg[:8] = times_exact(gy, fold)[:, :, :32]
    mean = jnp.where(rows((128, 128), 0) >> 2 == rows((128, 128), 1), 0.25, 0.0)
    msg[8] = exact(w[...], mean)[:, :32]


def join_kernel(own, r1, r2, r3, l3, l2, l1, field, w):
    first = jnp.concatenate([own[...], r1[...], r2[...], r3[...]], axis=2)
    second = jnp.concatenate([jnp.zeros((9, 8, 32), F32), l3[...], l2[...], l1[...]], axis=2)
    lane = rows((9, 8, 128), 2)
    main, rest = jnp.where(lane < 80, first, second), jnp.where(lane < 80, second, first)
    field[:, :, :128] = main[:8]
    field[:, :, 128:] = rest[:8]
    w[:, :128] = main[8]
    w[:, 128:] = rest[8]


def weights_2_kernel(w2, k2, k2u, m2, f2, k3, f3):
    iz = lax.axis_index("gz")
    band, op, step, factor = operators(w2[...], place_2, iz, 2, 69, S2)
    k2[...] = thrice(step)
    k2u[...] = thrice(step[:128, :128])
    m2[...] = thrice(op)
    f2[...] = jnp.broadcast_to(factor, (8, 256))
    mean = jnp.where(place_2(rows((256, 128), 0)) >> 1 == place_3(rows((256, 128), 1)), 0.5, 0.0)
    band, op, step, factor = operators(exact(w2[...], mean), place_3, iz, 3, 28, S3)
    k3[...] = thrice(step)
    f3[...] = jnp.broadcast_to(factor, (8, 128))


def up_kernel(
    r2x, ya, yb, yc, yd, k2, k2u, m2, f2, k3, f3,
    k1, f1, e1s, r1s, k0, m0, f0, e0s, r0s, stat0, stat1,
    sol, res, stat,
    ra, ea, eb, side2, gx2, r3, e3, side3, c3, cy2, ua, ub, side1, cy1, va, vb, side0, cy0, sol_v, res_v, sems,
):
    ix, iy, iz = lax.axis_index("gx"), lax.axis_index("gy"), lax.axis_index("gz")
    lane = rows((32, 128), 1)
    yrow = rows((32, 128), 0)
    for p in range(30):
        xr = ix * 8 + p - H2
        y = iy * 8 + yrow - H2
        ok = jnp.where(
            (y >= 0) & (y < NY // 4) & (yrow < 30), jnp.where((xr >= 0) & (xr < NX // 4), 1.0, 0.0), 0.0
        )
        full = jnp.concatenate([yc[p], ya[p], r2x[p], yb[p], yd[p], jnp.zeros((2, 256), F32)], axis=0)
        main, rest = full[:, :128] * ok, full[:, 128:] * ok
        ra[p, :, :128] = main
        ra[p, :, 128:] = rest
        ea[p, :, :128] = main * f2[0:1, :128]
        ea[p, :, 128:] = rest * f2[0:1, 128:]
        side2[p, :, :128] = ok * (f2[0:1, :128] * S2)
        side2[p, :, 128:] = ok * (f2[0:1, 128:] * S2)
    relax(ea, eb, 1, 29, 10, k2[...], lambda p, q: ea[p:q], side2)
    total = jnp.zeros((32, 128), F32)
    for p, q in chunks(2, 28, 13):
        mid, near = around(eb, p, q)
        value = ra[p:q] - times(mid, m2[...]) + S2 * near
        x = ix * 8 + rows(value.shape, 0) + (p - H2)
        y = iy * 8 + rows(value.shape, 1) - H2
        value = jnp.where((x >= 0) & (x < NX // 4) & (y >= 0) & (y < NY // 4), value, 0.0)
        ea[p:q] = value
        own = value[max(p, 11) - p : min(q, 19) - p, :, :128]
        total = total + jnp.sum(own * own, axis=0)
    keep = (yrow >= 11) & (yrow < 19) & (lane < 32)
    sum2 = jnp.sum(jnp.where(keep, total, 0.0))
    for i in range(12):
        value = ((ea[2 * i + 2] + ea[2 * i + 5]) + 3.0 * (ea[2 * i + 3] + ea[2 * i + 4])) * 0.125
        gx2[i, 0, :32] = value[:, :128]
        gx2[i, 1, :32] = value[:, 128:]
        gx2[i, 0, 32:] = jnp.zeros((8, 128), F32)
        gx2[i, 1, 32:] = jnp.zeros((8, 128), F32)
    gy = [
        jnp.concatenate([gx2[:, t, pl.ds(2 + a, 16, stride=2), :] for t in range(2)], axis=2) for a in range(4)
    ]
    gy = ((gy[0] + gy[3]) + 3.0 * (gy[1] + gy[2])) * 0.125
    fold = restrict_matrix(place_2, 256, place_3, 128, iz, 2, 65)
    mask = plane_mask((12, 16, 128), 3, ix, iy, H3)
    right3 = times_exact(gy, fold) * mask
    factor3 = f3[0:1, :].reshape(1, 1, 128)
    e3[...] = right3 * factor3
    side3[...] = mask * (factor3 * S3)
    c3[...] = jnp.zeros((12, 16, 128), F32)
    relax(e3, c3, 1, 11, 10, k3[...], lambda p, q: e3[p:q], side3)
    grow = prolong_matrix(place_3, 128, place_2, 128, iz, 2, 69)
    cz = times_exact(c3[...], grow)
    below, above = pltpu.roll(cz, 1, 1), pltpu.roll(cz, 15, 1)
    cy2[...] = jnp.zeros((12, 32, 128), F32)
    cy2[:, pl.ds(3, 12, stride=2), :] = (0.75 * cz + 0.25 * below)[:, :12]
    cy2[:, pl.ds(4, 12, stride=2), :] = (0.75 * cz + 0.25 * above)[:, :12]
    ua2, ub2 = r3, gx2
    fr2 = f2[0:1, :128].reshape(1, 1, 128)
    for xf in range(6, 24):
        f = xf - H2
        j = f // 2 + 4
        other = j - 1 if f % 2 == 0 else j + 1
        xr = ix * 8 + f
        y = iy * 8 + yrow - H2
        ok = jnp.where((y >= 0) & (y < NY // 4), jnp.where((xr >= 0) & (xr < NX // 4), 1.0, 0.0), 0.0)
        ea[xf, :, :128] = eb[xf, :, :128] + ok * (0.75 * cy2[j] + 0.25 * cy2[other])

    def relax_2(src, dst, a, b):
        for p, q in chunks(a, b, 8):
            mid = src[p:q, :, :128]
            near = (src[p + 1 : q + 1, :, :128] + src[p - 1 : q - 1, :, :128]) + (
                pltpu.roll(mid, 1, 1) + pltpu.roll(mid, 31, 1)
            )
            dst[p:q, :, :128] = times(mid, k2u[...]) + fr2 * ra[p:q, :, :128] + side2[p:q, :, :128] * near

    relax_2(ea, eb, 7, 23)
    relax_2(eb, ea, 8, 22)
    grow = prolong_matrix(place_2, 128, place_1, 128, iz, 1, 41)
    for p in range(14):
        r3[p] = ea[8 + p, :, :128]
    r3[...] = times_exact(r3[...], grow)
    cy1[...] = jnp.zeros((14, 32, 128), F32)
    cy1[:, pl.ds(1, 12, stride=2), :] = 0.75 * r3[:, 9:21, :] + 0.25 * r3[:, 8:20, :]
    cy1[:, pl.ds(2, 12, stride=2), :] = 0.75 * r3[:, 9:21, :] + 0.25 * r3[:, 10:22, :]
    fr1 = f1[0:1, :128].reshape(1, 1, 128)
    for xf in range(26):
        f = xf - H1
        xr = ix * 16 + f
        y = iy * 16 + yrow - H1
        ok = jnp.where((y >= 0) & (y < NY // 2), jnp.where((xr >= 0) & (xr < NX // 2), 1.0, 0.0), 0.0)
        side1[xf] = ok * (f1[0:1, :128] * S1)
        if 1 <= xf <= 24:
            j = f // 2 + 3
            other = j - 1 if f % 2 == 0 else j + 1
            ua[xf] = e1s[xf] + ok * (0.75 * cy1[j] + 0.25 * cy1[other])
    relax(ua, ub, 2, 24, 11, k1[...], lambda p, q: fr1 * r1s[p:q], side1)
    relax(ub, ua, 3, 23, 10, k1[...], lambda p, q: fr1 * r1s[p:q], side1)
    grow = prolong_matrix(place_1, 128, place_0, 256, iz, 0, 36)
    for p, q in chunks(0, 20, 10):
        cz = times_exact(ua[3 + p : 3 + q], grow)
        for t in range(2):
            part = cz[:, :, 128 * t : 128 * t + 128]
            cy0[p:q, t, pl.ds(0, 20, stride=2), :] = 0.75 * part[:, 3:23] + 0.25 * part[:, 2:22]
            cy0[p:q, t, pl.ds(1, 20, stride=2), :] = 0.75 * part[:, 3:23] + 0.25 * part[:, 4:24]
    fr0 = f0[0:1, :].reshape(1, 1, 256)
    for xf in range(40):
        f = xf - H0
        xr = ix * 32 + f
        y = iy * 32 + rows((40, 128), 0) - H0
        ok = jnp.where((y >= 0) & (y < NY), jnp.where((xr >= 0) & (xr < NX), 1.0, 0.0), 0.0)
        for t in range(2):
            part = slice(128 * t, 128 * t + 128)
            side0[xf, :, part] = ok * (f0[0:1, part] * S0)
            if 1 <= xf <= 38:
                j = f // 2 + 2
                other = j - 1 if f % 2 == 0 else j + 1
                va[xf, :, part] = e0s[xf, :, part] + ok * (0.75 * cy0[j, t] + 0.25 * cy0[other, t])
    relax(va, vb, 2, 38, 9, k0[...], lambda p, q: fr0 * r0s[p:q], side0)
    relax(vb, va, 3, 37, 9, k0[...], lambda p, q: fr0 * r0s[p:q], side0)
    total = jnp.zeros((32, 128), F32)
    last = m0[:, :128]
    sends = []
    for p, q in chunks(4, 36, 8):
        mid = va[p:q]
        flat = va[p:q, :, :128]
        near = (va[p + 1 : q + 1, :, :128] + va[p - 1 : q - 1, :, :128]) + (
            pltpu.roll(flat, 1, 1) + pltpu.roll(flat, 39, 1)
        )
        value = (r0s[p:q, :, :128] - times(mid, last) + S0 * near)[:, 4:36]
        part = slice(p - 4, q - 4)
        res_v[part] = value
        sol_v[part] = va[p:q, 4:36, :128]
        total = total + jnp.sum(value * value, axis=0)
        for i, (src, dst) in enumerate(((sol_v, sol), (res_v, res))):
            sends.append(pltpu.make_async_copy(src.at[part], dst.at[part], sems.at[i, p // 8]))
            sends[-1].start()
    sum3 = jnp.sum(total)
    tile = rows((1, 128), 1)
    stat[...] = jnp.where(
        tile == 0, stat0[0:1], jnp.where(tile == 1, stat1[0:1], jnp.where(tile == 2, sum2, jnp.where(tile == 3, sum3, 0.0)))
    )
    for send in sends:
        send.wait()


def shift(x, axis, k):
    n = lax.axis_size(axis)
    return lax.ppermute(x, axis, [((i + k) % n, i) for i in range(n)])


def swap(x, axis, flip):
    return lax.ppermute(x, axis, [(i ^ flip, i) for i in range(lax.axis_size(axis))])


def f32(*shape):
    return pltpu.VMEM(shape, F32)


def bf16(*shape):
    return pltpu.VMEM(shape, BF16)


def scratch(*shape):
    return pltpu.VMEM(shape, F32)


def call(kernel, outs, scratches, name, limit=16, away=()):
    def run(*operands):
        operands = [x if x is None else pltpu.with_memory_space_constraint(x, pltpu.VMEM) for x in operands]
        return pl.pallas_call(
            kernel,
            out_shape=[jax.ShapeDtypeStruct(o.shape, F32) if i in away else o for i, o in enumerate(outs)],
            in_specs=[pl.BlockSpec(memory_space=pltpu.VMEM)] * len(operands),
            out_specs=[pl.BlockSpec(memory_space=pl.ANY if i in away else pltpu.VMEM) for i in range(len(outs))],
            scratch_shapes=scratches,
            compiler_params=pltpu.CompilerParams(vmem_limit_bytes=limit * 2**20),
            name=name,
        )(*operands)

    return run


def pack(width, reach, count, n, height, groups, parts, extra, name):
    def kernel(*refs):
        if extra is None:
            refs = refs[:5] + (None,) + refs[5:]
        pack_kernel(width, reach, count, n, *refs)

    outs = [f32(n + 2 * reach, height, 128), f32(groups, height, 128), f32(groups, height, 128)]
    return call(kernel, outs, [], name)(*parts, *(() if extra is None else (extra,)))


def sides(block, first, last, low, high, reach):
    n = block.shape[0]
    xlo = shift(last, "gx", -1)
    xhi = shift(first, "gx", 1)
    top = jnp.concatenate([xlo[:, n - reach :], high, xhi[:, n - reach :]], axis=0)
    bottom = jnp.concatenate([xlo[:, :reach], low, xhi[:, :reach]], axis=0)
    return block, xlo, xhi, shift(top, "gy", -1), shift(bottom, "gy", 1)


def body(data, weights):
    slab = f32(H0, 32, 128), f32(H0, 32, 128), f32(32, H0, 128), f32(32, H0, 128)
    start = pl.pallas_call(
        prepare_kernel,
        out_shape=[f32(32, 32, 128), *slab],
        in_specs=[pl.BlockSpec(memory_space=pltpu.VMEM)],
        out_specs=[pl.BlockSpec(memory_space=pltpu.VMEM)] * 5,
        name="prepare",
    )(data)
    dxy, to_left, to_right = pack(36, H0, 128, 32, 40, 15, sides(*start, H0), weights, "pack_data")
    from_right, from_left = shift(to_left, "gz", 1), shift(to_right, "gz", -1)
    b0, k0, m0, f0 = call(
        weights_0_kernel, [bf16(768, 256), bf16(768, 256), bf16(768, 256), f32(8, 256)], [], "weights_0"
    )(from_left, weights, from_right)
    k1, k1u, m1, f1 = call(
        weights_1_kernel, [bf16(768, 128), bf16(384, 128), bf16(384, 128), f32(8, 256)], [], "weights_1"
    )(from_left, weights, from_right)
    big = (40, 40, 256)
    r1, r1_top, r1_bottom, e0s, r0s, stat0 = call(
        down_0_kernel,
        [f32(16, 16, 64), f32(16, H1, 64), f32(16, H1, 64), f32(*big), f32(*big), f32(8, 128)],
        [scratch(*big), scratch(*big), scratch(*big), scratch(*big), scratch(16, 2, 40, 128)],
        "down_0",
    )(dxy, from_right, from_left, b0, k0, m0, f0)
    rxy, to_left, to_right = pack(
        37, H1, 64, 16, 32, 9, sides(r1, r1[:H1], r1[16 - H1 :], r1_bottom, r1_top, H1), None, "pack_r1"
    )
    from_right, from_left = shift(to_left, "gz", 1), shift(to_right, "gz", -1)
    mid = (26, 32, 128)
    msg, e1s, r1s, stat1 = call(
        down_1_kernel,
        [f32(9, 8, 32), f32(*mid), f32(*mid), f32(8, 128)],
        [scratch(*mid), scratch(*mid), scratch(*mid), scratch(*mid), scratch(8, 32, 128)],
        "down_1",
    )(rxy, from_right, from_left, k1, m1, f1, weights)
    near = {k: shift(msg, "gz", k) for k in (1, -1, 2, -2, 3, -3)}
    r2z, wide2 = call(join_kernel, [f32(8, 8, 256), f32(8, 256)], [], "join")(
        msg, near[1], near[2], near[3], near[-3], near[-2], near[-1]
    )
    k2, k2u, m2, f2, k3, f3 = call(
        weights_2_kernel,
        [bf16(768, 256), bf16(384, 128), bf16(768, 256), f32(8, 256), bf16(384, 128), f32(8, 128)],
        [], "weights_coarse",
    )(wide2)
    x1, x2, x3 = (shift(r2z, "gx", k) for k in (1, 2, 3))
    r2x = jnp.concatenate([x2[5:], x3, r2z, x1, x2[:3]], axis=0)
    ya, yb = shift(r2x, "gy", -1), shift(r2x, "gy", 1)
    yc, yd = shift(r2x[:, 5:], "gy", -2), shift(r2x[:, :3], "gy", 2)
    lev2 = (30, 32, 256)
    sol, res, stat = call(
        up_kernel,
        [f32(32, 32, 128), f32(32, 32, 128), f32(1, 128)],
        [
            scratch(*lev2), scratch(*lev2), scratch(*lev2), scratch(*lev2), scratch(12, 2, 40, 128),
            scratch(14, 32, 128), scratch(12, 16, 128), scratch(12, 16, 128), scratch(12, 16, 128),
            scratch(12, 32, 128), scratch(*mid), scratch(*mid), scratch(*mid), scratch(14, 32, 128),
            scratch(*big), scratch(*big), scratch(*big), scratch(20, 2, 40, 128), scratch(32, 32, 128), scratch(32, 32, 128), pltpu.SemaphoreType.DMA((2, 5)),
        ],
        "up", 24, (0, 1),
    )(r2x, ya, yb, yc, yd, k2, k2u, m2, f2, k3, f3, k1u, f1, e1s, r1s, k0, m0, f0, e0s, r0s, stat0, stat1)
    t = stat
    for axis, flips in (("gy", (1,)), ("gx", (1, 2, 3)), ("gy", (2, 4, 6)), ("gz", (1, 2, 3)), ("gz", (7,))):
        others = [swap(t, axis, f) for f in flips]
        t = t + others[0]
        if len(others) > 1:
            t = t + (others[1] + others[2])
    cells = jnp.array([NX * NY * NZ >> (3 * k) for k in (0, 1, 2, 0)], F32)
    return sol, res, jnp.sqrt(t[0, :4] / cells)


def solution(mesh):
    placed = (P("gx", "gy", "gz"), P(None, "gz"))
    return jax.shard_map(
        body,
        mesh=mesh,
        in_specs=placed,
        out_specs=(P("gx", "gy", "gz"), P("gx", "gy", "gz"), P()),
        check_vma=False,
    )
```

```python
import jax
import jax.numpy as jnp
from jax import lax
from jax.sharding import PartitionSpec as P
from jax.experimental import pallas as pl
from jax.experimental.pallas import tpu as pltpu

OFFSETS = (-4, -3, -2, -1, 1, 2, 3, 4)
RELAX = 0.45
NX, NY, NZ = 128, 256, 1024
F32, BF16 = jnp.float32, jnp.bfloat16
H0, H1, H2, H3 = 4, 5, 11, 4
S0, S1, S2, S3 = 1.0, 0.25, 0.0625, 0.015625
SLOT = 40
TAILS = {1: (0, 28), 2: (56, 20), 3: (96, 12), 4: (120, 4)}


def place_0(p):
    return jnp.where(p < 192, p, p - 256)


def place_1(p):
    lane = p & 127
    return jnp.where((lane < 96) == (p < 128), lane, lane - 128)


def place_2(p):
    lane = p & 127
    return jnp.where((lane < 80) == (p < 128), lane, lane - 128)


def place_3(p):
    return jnp.where(p < 64, p, p - 128)


def inside(z, iz, level, reach):
    count = 128 >> level
    glob = iz * count + z
    return (z >= -reach) & (z < count + reach) & (glob >= 0) & (glob < (NZ >> level))


def rows(shape, dim):
    return lax.broadcasted_iota(jnp.int32, shape, dim)


def halves(a):
    hi = a.astype(BF16)
    return hi, (a - hi.astype(F32)).astype(BF16)


def thrice(matrix):
    hi, lo = halves(matrix)
    return jnp.concatenate([hi, hi, lo], axis=0)


def times(field, matrix):
    shape = field.shape
    hi, lo = halves(field.reshape(shape[0] * shape[1], shape[2]))
    out = jnp.dot(jnp.concatenate([hi, lo, hi], axis=1), matrix, preferred_element_type=F32)
    return out.reshape(shape[0], shape[1], matrix.shape[1])


def times_exact(field, matrix):
    shape = field.shape
    hi, lo = halves(field.reshape(shape[0] * shape[1], shape[2]))
    out = jnp.dot(jnp.concatenate([hi, lo], axis=1), matrix, preferred_element_type=F32)
    return out.reshape(shape[0], shape[1], matrix.shape[1])


def exact(a, b):
    return jnp.dot(a, b, precision=lax.Precision.HIGHEST, preferred_element_type=F32)


def operators(w, place, iz, level, reach, stiffness):
    n = w.shape[1]
    zk = place(rows((n, n), 0))
    zn = place(rows((n, n), 1))
    both = inside(zk, iz, level, reach) & inside(zn, iz, level, reach)
    gap = jnp.where(both, zk - zn, 99)
    band = jnp.where(gap == 0, 1.0, 0.0)
    eye = jnp.where(rows((n, n), 0) == rows((n, n), 1), 1.0, 0.0)
    for j, offset in enumerate(OFFSETS):
        band = jnp.where(gap == offset, w[j : j + 1, :], band)
    gram = lax.dot_general(
        band, band, (((1,), (1,)), ((), ())), precision=lax.Precision.HIGHEST, preferred_element_type=F32
    )
    diag = jnp.sum(gram * eye, axis=0, keepdims=True) + 6.0 * stiffness
    line = inside(place(rows((1, n), 1)), iz, level, reach)
    factor = jnp.where(line, RELAX / diag, 0.0)
    op = gram + stiffness * (6.0 * eye - jnp.where((gap == 1) | (gap == -1), 1.0, 0.0))
    return band, op, eye - op * factor, factor


def restrict_matrix(place_f, n_f, place_c, n_c, iz, level, reach):
    zf = place_f(rows((n_f, n_c), 0))
    zc = place_c(rows((n_f, n_c), 1))
    gap = zf - 2 * zc
    near = jnp.where((gap == 0) | (gap == 1), 0.375, 0.0) + jnp.where((gap == -1) | (gap == 2), 0.125, 0.0)
    m = jnp.where(inside(zf, iz, level, reach), near, 0.0).astype(BF16)
    return jnp.concatenate([m, m], axis=0)


def prolong_matrix(place_c, n_c, place_f, n_f, iz, level, reach):
    zc = place_c(rows((n_c, n_f), 0))
    zf = place_f(rows((n_c, n_f), 1))
    gap = zf - 2 * zc
    near = jnp.where((gap == 0) | (gap == 1), 0.75, 0.0) + jnp.where((gap == -1) | (gap == 2), 0.25, 0.0)
    m = jnp.where(inside(zf, iz, level, reach), near, 0.0).astype(BF16)
    return jnp.concatenate([m, m], axis=0)


def plane_mask(shape, level, ix, iy, reach):
    x = ix * (32 >> level) + rows(shape, 0) - reach
    y = iy * (32 >> level) + rows(shape, 1) - reach
    ok = (x >= 0) & (x < (NX >> level)) & (y >= 0) & (y < (NY >> level))
    return jnp.where(ok, 1.0, 0.0)


def around(ref, a, b):
    mid = ref[a:b]
    count = mid.shape[1]
    return mid, (ref[a + 1 : b + 1] + ref[a - 1 : b - 1]) + (pltpu.roll(mid, 1, 1) + pltpu.roll(mid, count - 1, 1))


def chunks(a, b, step):
    return [(c, min(c + step, b)) for c in range(a, b, step)]


def relax(src, dst, a, b, step, matrix, right, side):
    for p, q in chunks(a, b, step):
        mid, near = around(src, p, q)
        dst[p:q] = times(mid, matrix) + right(p, q) + side[p:q] * near


def pack_lanes(planes, height, width, count, to_left, to_right):
    lane = rows((height, 128), 1)
    for g in range(-(-len(planes) // 3)):
        left, right = None, None
        for i, value in enumerate(planes[3 * g : 3 * g + 3]):
            a = pltpu.roll(value, SLOT * i, 1) if i else value
            b = pltpu.roll(value, (SLOT * i + width - count) % 128, 1)
            left = a if i == 0 else jnp.where(lane < SLOT * i, left, a)
            right = b if i == 0 else jnp.where(lane < SLOT * i, right, b)
        to_left[g] = left
        to_right[g] = right


def prepare_kernel(data, weights, own, to_left, to_right):
    own[...] = data[...]
    pack_lanes([data[p] for p in range(32)], 32, 36, 128, to_left, to_right)
    for out in (to_left, to_right):
        out[11] = jnp.concatenate([weights[...], jnp.zeros((24, 128), F32)], axis=0)


def spread_0_kernel(own, from_right, from_left, tail, first, last):
    lane = rows((32, 128), 1)
    packed = [jnp.zeros((32, 128), F32)] * 2
    for p in range(32):
        group, i = divmod(p, 3)
        right = pltpu.roll(from_right[group], 128 - SLOT * i, 1) if i else from_right[group]
        left = pltpu.roll(from_left[group], (92 - SLOT * i) % 128, 1)
        value = jnp.where(lane < 36, right, jnp.where(lane >= 92, left, 0.0))
        tail[p] = value
        for side, far in ((0, p + 1), (1, 32 - p)):
            if far <= H0:
                begin, reach = TAILS[far]
                moved = pltpu.roll(value, begin + reach, 1)
                packed[side] = jnp.where((lane >= begin) & (lane < begin + 2 * reach), moved, packed[side])
    first[:H0] = own[:H0]
    first[H0] = packed[0]
    last[:H0] = own[32 - H0 :]
    last[H0] = packed[1]


def edges_0_kernel(own, tail, xlo, xhi, low, high):
    lane = rows((4, 128), 1)

    def ends(ref, p):
        value = ref[p]
        return value[:H0], value[32 - H0 :]

    def tails(p):
        if H0 <= p < 32 + H0:
            return ends(tail, p - H0)
        source = xlo if p < H0 else xhi
        begin, reach = TAILS[H0 - p if p < H0 else p - 31 - H0]
        out = []
        for value in ends(source, H0):
            moved = pltpu.roll(value, (128 - begin - reach) % 128, 1)
            out.append(jnp.where((lane < reach) | (lane >= 128 - reach), moved, 0.0))
        return out

    kept = None
    for p in range(40):
        if p < H0:
            a, b = ends(xlo, p)
        elif p < 32 + H0:
            a, b = ends(own, p - H0)
        else:
            a, b = ends(xhi, p - 32 - H0)
        low[p] = a
        high[p] = b
        moved = [pltpu.roll(v, 28 if p % 2 == 0 else 92, 1) for v in tails(p)]
        if p % 2 == 0:
            kept = moved
        else:
            low[40 + p // 2] = jnp.where(lane < 64, kept[0], moved[0])
            high[40 + p // 2] = jnp.where(lane < 64, kept[1], moved[1])


def gather_0_kernel(own, tail, xlo, xhi, field):
    ix = lax.axis_index("gx")
    lane = rows((32, 128), 1)
    for p in range(40):
        if H0 <= p < 32 + H0:
            field[p, 4:36, :128] = own[p - H0]
            field[p, 4:36, 128:] = tail[p - H0]
        else:
            source, q = (xlo, p) if p < H0 else (xhi, p - 32 - H0)
            begin, reach = TAILS[H0 - p if p < H0 else p - 31 - H0]
            xr = ix * 32 + p - H0
            ok = jnp.where((xr >= 0) & (xr < NX), 1.0, 0.0)
            moved = pltpu.roll(source[H0], (128 - begin - reach) % 128, 1)
            field[p, 4:36, :128] = source[q] * ok
            field[p, 4:36, 128:] = jnp.where((lane < reach) | (lane >= 128 - reach), moved, 0.0) * ok
        field[p, :4] = jnp.zeros((4, 256), F32)
        field[p, 36:] = jnp.zeros((4, 256), F32)


def weights_0_kernel(left, own, right, b0, k0, m0, f0):
    iz = lax.axis_index("gz")
    lane = rows((8, 128), 1)
    laid = jnp.concatenate([own[...], jnp.where(lane < 64, right[11, :8], left[11, :8])], axis=1)
    band, op, step, factor = operators(laid, place_0, iz, 0, 36, S0)
    b0[...] = thrice(jnp.transpose(band))
    k0[...] = thrice(step)
    m0[...] = thrice(op)
    f0[...] = jnp.broadcast_to(factor, (8, 256))


def weights_1_kernel(left, own, right, k1, k1u, m1, f1):
    iz = lax.axis_index("gz")
    wide = jnp.concatenate([left[11, :8], own[...], right[11, :8]], axis=1)
    mean = jnp.where((rows((384, 256), 0) - 128) >> 1 == place_1(rows((384, 256), 1)), 0.5, 0.0)
    band, op, step, factor = operators(exact(wide, mean), place_1, iz, 1, 41, S1)
    k1[...] = thrice(step[:, :128])
    k1u[...] = thrice(step[:128, :128])
    m1[...] = thrice(op[:128, :128])
    f1[...] = jnp.broadcast_to(factor, (8, 256))


def spread_1_kernel(own, from_right, from_left, main, rest, first, last):
    lane = rows((16, 128), 1)
    for p in range(16):
        group, i = divmod(p, 3)
        right = pltpu.roll(from_right[group], (64 - SLOT * i) % 128, 1)
        left = pltpu.roll(from_left[group], (91 - SLOT * i) % 128, 1)
        one = jnp.where(lane < 64, own[p], jnp.where(lane < 101, right, 0.0))
        two = jnp.where(lane >= 91, left, 0.0)
        main[p] = jnp.where(lane < 96, one, two)
        rest[p] = jnp.where(lane < 96, two, one)
    first[:H1] = main[:H1]
    first[H1] = rest[0]
    last[:H1] = main[16 - H1 :]
    last[H1] = rest[15]


def edges_1_kernel(main, rest, xlo, xhi, low, high):
    for p in range(26):
        if p < H1:
            value, tail = xlo[p], xlo[H1] if p == H1 - 1 else None
        elif p < 16 + H1:
            value, tail = main[p - H1], rest[p - H1]
        else:
            value, tail = xhi[p - 16 - H1], xhi[H1] if p == 16 + H1 else None
        low[p, :H1] = value[:H1]
        high[p, :H1] = value[16 - H1 :]
        none = jnp.zeros((8 - H1, 128), F32)
        low[p, H1:] = none
        high[p, H1:] = none
        if tail is not None:
            low[p, H1 : H1 + 1] = tail[0:1]
            high[p, H1 : H1 + 1] = tail[15:16]


def down_0_kernel(
    field, ylo, yhi, b0, k0, m0, f0, r1, to_left, to_right, e_out, r_out, stat, d, e0, side, g, gx
):
    ix, iy, iz = lax.axis_index("gx"), lax.axis_index("gy"), lax.axis_index("gz")
    low_ok = jnp.where(iy > 0, 1.0, 0.0)
    high_ok = jnp.where(iy < 7, 1.0, 0.0)
    y = iy * 32 + rows((40, 256), 0) - H0
    column = jnp.where((y >= 0) & (y < NY), f0[0:1, :] * S0, 0.0)
    lane = rows((4, 128), 1)
    for p in range(40):
        xr = ix * 32 + p - H0
        ok = jnp.where((xr >= 0) & (xr < NX), 1.0, 0.0)
        d[p, 4:36] = field[p, 4:36]
        for edge, part, good in ((ylo, slice(0, 4), low_ok), (yhi, slice(36, 40), high_ok)):
            moved = pltpu.roll(edge[40 + p // 2], 100 if p % 2 == 0 else 36, 1)
            d[p, part, :128] = edge[p] * (ok * good)
            d[p, part, 128:] = jnp.where((lane < 28) | (lane >= 100), moved, 0.0) * (ok * good)
        side[p] = column * ok
    factor = f0[0:1, :].reshape(1, 1, 256)
    for p, q in chunks(0, 40, 8):
        r = times(d[p:q], b0[...])
        r_out[p:q] = r
        e0[p:q] = r * factor
    relax(e0, e_out, 1, 39, 10, k0[...], lambda p, q: e0[p:q], side)
    e_out[0] = jnp.zeros((40, 256), F32)
    e_out[39] = jnp.zeros((40, 256), F32)
    total = jnp.zeros((40, 128), F32)
    for p, q in chunks(3, 37, 9):
        mid, near = around(e_out, p, q)
        value = r_out[p:q] - times(mid, m0[...]) + S0 * near
        x = ix * 32 + rows(value.shape, 0) + (p - H0)
        y = iy * 32 + rows(value.shape, 1) - H0
        value = jnp.where((x >= 0) & (x < NX) & (y >= 0) & (y < NY), value, 0.0)
        g[p:q] = value
        own = value[max(p, 4) - p : min(q, 36) - p, :, :128]
        total = total + jnp.sum(own * own, axis=0)
    row = rows((40, 128), 0)
    stat[...] = jnp.full((8, 128), jnp.sum(jnp.where((row >= 4) & (row < 36), total, 0.0)), F32)
    for i in range(16):
        value = ((g[2 * i + 3] + g[2 * i + 6]) + 3.0 * (g[2 * i + 4] + g[2 * i + 5])) * 0.125
        gx[i, 0] = value[:, :128]
        gx[i, 1] = value[:, 128:]
    gy = [
        jnp.concatenate([gx[:, t, pl.ds(3 + a, 16, stride=2), :] for t in range(2)], axis=2) for a in range(4)
    ]
    gy = ((gy[0] + gy[3]) + 3.0 * (gy[1] + gy[2])) * 0.125
    fold = restrict_matrix(place_0, 256, lambda q: q, 128, iz, 0, 36)
    out = times_exact(gy, fold)
    r1[...] = out
    pack_lanes([out[i] for i in range(16)], 16, 37, 64, to_left, to_right)


def down_1_kernel(wide, tail, xlo, xhi, ylo, yhi, k1, m1, f1, w, msg, e_out, r_out, stat, e0, e0b, side, g, gx):
    ix, iy, iz = lax.axis_index("gx"), lax.axis_index("gy"), lax.axis_index("gz")
    lane = rows((32, 128), 1)
    yrow = rows((32, 128), 0)
    y = iy * 16 + yrow - H1
    inner = jnp.where((y >= 0) & (y < NY // 2) & (yrow < 26), 1.0, 0.0)
    for p in range(26):
        xr = ix * 16 + p - H1
        ok = inner * jnp.where((xr >= 0) & (xr < NX // 2), 1.0, 0.0)
        if p < H1:
            value, extra = xlo[p], xlo[H1] if p == H1 - 1 else jnp.zeros((16, 128), F32)
        elif p < 16 + H1:
            value, extra = wide[p - H1], tail[p - H1]
        else:
            value, extra = xhi[p - 16 - H1], xhi[H1] if p == 16 + H1 else jnp.zeros((16, 128), F32)
        main = jnp.concatenate([ylo[p, :H1], value, yhi[p, :H1], jnp.zeros((6, 128), F32)], axis=0) * ok
        rest = jnp.concatenate(
            [jnp.zeros((4, 128), F32), ylo[p, H1 : H1 + 1], extra, yhi[p, H1 : H1 + 1], jnp.zeros((10, 128), F32)],
            axis=0,
        ) * ok
        r_out[p] = main
        e0[p] = main * f1[0:1, :128]
        e0b[p] = rest * f1[0:1, 128:]
        side[p] = ok * (f1[0:1, :128] * S1)
    for p, q in chunks(1, 25, 8):
        mid, near = around(e0, p, q)
        both = jnp.concatenate([mid, e0b[p:q]], axis=2)
        e_out[p:q] = times(both, k1[...]) + mid + side[p:q] * near
    e_out[0] = jnp.zeros((32, 128), F32)
    e_out[25] = jnp.zeros((32, 128), F32)
    total = jnp.zeros((32, 128), F32)
    for p, q in chunks(4, 22, 9):
        mid, near = around(e_out, p, q)
        value = r_out[p:q] - times(mid, m1[...]) + S1 * near
        x = ix * 16 + rows(value.shape, 0) + (p - H1)
        y = iy * 16 + rows(value.shape, 1) - H1
        value = jnp.where((x >= 0) & (x < NX // 2) & (y >= 0) & (y < NY // 2), value, 0.0)
        g[p:q] = value
        own = value[max(p, 5) - p : min(q, 21) - p]
        total = total + jnp.sum(own * own, axis=0)
    row = rows((32, 128), 0)
    keep = (row >= 5) & (row < 21) & (lane < 64)
    stat[...] = jnp.full((8, 128), jnp.sum(jnp.where(keep, total, 0.0)), F32)
    for i in range(8):
        gx[i] = ((g[2 * i + 4] + g[2 * i + 7]) + 3.0 * (g[2 * i + 5] + g[2 * i + 6])) * 0.125
    gy = [gx[:, pl.ds(4 + a, 8, stride=2), :] for a in range(4)]
    gy = ((gy[0] + gy[3]) + 3.0 * (gy[1] + gy[2])) * 0.125
    fold = restrict_matrix(place_1, 128, lambda q: q, 128, iz, 1, 32)
    out = times_exact(gy, fold)[:, :, :32]
    for k in range(2):
        msg[k] = jnp.concatenate([out[4 * k + i] for i in range(4)], axis=1)
    mean = jnp.where(rows((128, 128), 0) >> 2 == rows((128, 128), 1), 0.25, 0.0)
    msg[2] = exact(w[...], mean)


def join_kernel(own, r1, r2, r3, l3, l2, l1, both, w):
    lane = rows((8, 128), 1)
    blocks = (own, r1, r2, r3), (None, l3, l2, l1)
    for p in range(9):
        k, i = divmod(p, 4)
        part = slice(32 * i, 32 * i + 32)
        first, second = (
            jnp.concatenate([jnp.zeros((8, 32), F32) if b is None else b[k, :, part] for b in group], axis=1)
            for group in blocks
        )
        main, rest = jnp.where(lane < 80, first, second), jnp.where(lane < 80, second, first)
        if p < 8:
            both[p] = main
            both[8 + p] = rest
        else:
            w[:, :128] = main
            w[:, 128:] = rest


def edges_2_kernel(own, x1, x2, x3, near, low, high):
    near[:3] = x2[5:]
    near[3:11] = x3[:8]
    near[11:19] = own[:8]
    near[19:27] = x1[:8]
    near[27:30] = x2[:3]
    near[30:36] = x3[10:]
    near[36:44] = own[8:]
    near[44:50] = x1[8:14]
    for i in range(18):
        value = near[i + 6]
        low[i] = value[:3]
        high[i] = value[5:]


def weights_2_kernel(w2, k2, k2u, m2, f2, k3, f3):
    iz = lax.axis_index("gz")
    band, op, step, factor = operators(w2[...], place_2, iz, 2, 69, S2)
    k2[...] = thrice(step)
    k2u[...] = thrice(step[:128, :128])
    m2[...] = thrice(op)
    f2[...] = jnp.broadcast_to(factor, (8, 256))
    mean = jnp.where(place_2(rows((256, 128), 0)) >> 1 == place_3(rows((256, 128), 1)), 0.5, 0.0)
    band, op, step, factor = operators(exact(w2[...], mean), place_3, iz, 3, 28, S3)
    k3[...] = thrice(step)
    f3[...] = jnp.broadcast_to(factor, (8, 128))


def up_kernel(
    r2x, ya, yb, yc, yd, k2, k2u, m2, f2, k3, f3,
    k1, f1, e1s, r1s, k0, m0, f0, e0s, r0s, stat0, stat1,
    sol, res, stat,
    ra, ea, eb, side2, gx2, r3, e3, side3, c3, cy2, ua, ub, side1, cy1, va, vb, side0, cy0,
):
    ix, iy, iz = lax.axis_index("gx"), lax.axis_index("gy"), lax.axis_index("gz")
    lane = rows((32, 128), 1)
    yrow = rows((32, 128), 0)
    for p in range(30):
        xr = ix * 8 + p - H2
        y = iy * 8 + yrow - H2
        ok = jnp.where(
            (y >= 0) & (y < NY // 4) & (yrow < 30), jnp.where((xr >= 0) & (xr < NX // 4), 1.0, 0.0), 0.0
        )
        three, two = jnp.zeros((3, 128), F32), jnp.zeros((2, 128), F32)
        far = 6 <= p < 24
        main = jnp.concatenate(
            [yc[p - 6] if far else three, ya[p], r2x[p], yb[p], yd[p - 6] if far else three, two], axis=0
        ) * ok
        rest = jnp.zeros((32, 128), F32)
        if 5 <= p < 25:
            rest = jnp.concatenate([three, ya[p + 25], r2x[p + 25], yb[p + 25], three, two], axis=0) * ok
        ra[p, :, :128] = main
        ra[p, :, 128:] = rest
        ea[p, :, :128] = main * f2[0:1, :128]
        ea[p, :, 128:] = rest * f2[0:1, 128:]
        side2[p, :, :128] = ok * (f2[0:1, :128] * S2)
        side2[p, :, 128:] = ok * (f2[0:1, 128:] * S2)
    relax(ea, eb, 1, 29, 10, k2[...], lambda p, q: ea[p:q], side2)
    total = jnp.zeros((32, 128), F32)
    for p, q in chunks(2, 28, 13):
        mid, near = around(eb, p, q)
        value = ra[p:q] - times(mid, m2[...]) + S2 * near
        x = ix * 8 + rows(value.shape, 0) + (p - H2)
        y = iy * 8 + rows(value.shape, 1) - H2
        value = jnp.where((x >= 0) & (x < NX // 4) & (y >= 0) & (y < NY // 4), value, 0.0)
        ea[p:q] = value
        own = value[max(p, 11) - p : min(q, 19) - p, :, :128]
        total = total + jnp.sum(own * own, axis=0)
    keep = (yrow >= 11) & (yrow < 19) & (lane < 32)
    sum2 = jnp.sum(jnp.where(keep, total, 0.0))
    for i in range(12):
        value = ((ea[2 * i + 2] + ea[2 * i + 5]) + 3.0 * (ea[2 * i + 3] + ea[2 * i + 4])) * 0.125
        gx2[i, 0, :32] = value[:, :128]
        gx2[i, 1, :32] = value[:, 128:]
        gx2[i, 0, 32:] = jnp.zeros((8, 128), F32)
        gx2[i, 1, 32:] = jnp.zeros((8, 128), F32)
    gy = [
        jnp.concatenate([gx2[:, t, pl.ds(2 + a, 16, stride=2), :] for t in range(2)], axis=2) for a in range(4)
    ]
    gy = ((gy[0] + gy[3]) + 3.0 * (gy[1] + gy[2])) * 0.125
    fold = restrict_matrix(place_2, 256, place_3, 128, iz, 2, 65)
    mask = plane_mask((12, 16, 128), 3, ix, iy, H3)
    right3 = times_exact(gy, fold) * mask
    factor3 = f3[0:1, :].reshape(1, 1, 128)
    e3[...] = right3 * factor3
    side3[...] = mask * (factor3 * S3)
    c3[...] = jnp.zeros((12, 16, 128), F32)
    relax(e3, c3, 1, 11, 10, k3[...], lambda p, q: e3[p:q], side3)
    grow = prolong_matrix(place_3, 128, place_2, 128, iz, 2, 69)
    cz = times_exact(c3[...], grow)
    below, above = pltpu.roll(cz, 1, 1), pltpu.roll(cz, 15, 1)
    cy2[...] = jnp.zeros((12, 32, 128), F32)
    cy2[:, pl.ds(3, 12, stride=2), :] = (0.75 * cz + 0.25 * below)[:, :12]
    cy2[:, pl.ds(4, 12, stride=2), :] = (0.75 * cz + 0.25 * above)[:, :12]
    ua2, ub2 = r3, gx2
    fr2 = f2[0:1, :128].reshape(1, 1, 128)
    for xf in range(6, 24):
        f = xf - H2
        j = f // 2 + 4
        other = j - 1 if f % 2 == 0 else j + 1
        xr = ix * 8 + f
        y = iy * 8 + yrow - H2
        ok = jnp.where((y >= 0) & (y < NY // 4), jnp.where((xr >= 0) & (xr < NX // 4), 1.0, 0.0), 0.0)
        ea[xf, :, :128] = eb[xf, :, :128] + ok * (0.75 * cy2[j] + 0.25 * cy2[other])

    def relax_2(src, dst, a, b):
        for p, q in chunks(a, b, 8):
            mid = src[p:q, :, :128]
            near = (src[p + 1 : q + 1, :, :128] + src[p - 1 : q - 1, :, :128]) + (
                pltpu.roll(mid, 1, 1) + pltpu.roll(mid, 31, 1)
            )
            dst[p:q, :, :128] = times(mid, k2u[...]) + fr2 * ra[p:q, :, :128] + side2[p:q, :, :128] * near

    relax_2(ea, eb, 7, 23)
    relax_2(eb, ea, 8, 22)
    grow = prolong_matrix(place_2, 128, place_1, 128, iz, 1, 41)
    for p in range(14):
        r3[p] = ea[8 + p, :, :128]
    r3[...] = times_exact(r3[...], grow)
    cy1[...] = jnp.zeros((14, 32, 128), F32)
    cy1[:, pl.ds(1, 12, stride=2), :] = 0.75 * r3[:, 9:21, :] + 0.25 * r3[:, 8:20, :]
    cy1[:, pl.ds(2, 12, stride=2), :] = 0.75 * r3[:, 9:21, :] + 0.25 * r3[:, 10:22, :]
    fr1 = f1[0:1, :128].reshape(1, 1, 128)
    for xf in range(26):
        f = xf - H1
        xr = ix * 16 + f
        y = iy * 16 + yrow - H1
        ok = jnp.where((y >= 0) & (y < NY // 2), jnp.where((xr >= 0) & (xr < NX // 2), 1.0, 0.0), 0.0)
        side1[xf] = ok * (f1[0:1, :128] * S1)
        if 1 <= xf <= 24:
            j = f // 2 + 3
            other = j - 1 if f % 2 == 0 else j + 1
            ua[xf] = e1s[xf] + ok * (0.75 * cy1[j] + 0.25 * cy1[other])
    relax(ua, ub, 2, 24, 11, k1[...], lambda p, q: fr1 * r1s[p:q], side1)
    relax(ub, ua, 3, 23, 10, k1[...], lambda p, q: fr1 * r1s[p:q], side1)
    grow = prolong_matrix(place_1, 128, place_0, 256, iz, 0, 36)
    for p, q in chunks(0, 20, 10):
        cz = times_exact(ua[3 + p : 3 + q], grow)
        for t in range(2):
            part = cz[:, :, 128 * t : 128 * t + 128]
            cy0[p:q, t, pl.ds(0, 20, stride=2), :] = 0.75 * part[:, 3:23] + 0.25 * part[:, 2:22]
            cy0[p:q, t, pl.ds(1, 20, stride=2), :] = 0.75 * part[:, 3:23] + 0.25 * part[:, 4:24]
    fr0 = f0[0:1, :].reshape(1, 1, 256)
    for xf in range(40):
        f = xf - H0
        xr = ix * 32 + f
        y = iy * 32 + rows((40, 128), 0) - H0
        ok = jnp.where((y >= 0) & (y < NY), jnp.where((xr >= 0) & (xr < NX), 1.0, 0.0), 0.0)
        for t in range(2):
            part = slice(128 * t, 128 * t + 128)
            side0[xf, :, part] = ok * (f0[0:1, part] * S0)
            if 1 <= xf <= 38:
                j = f // 2 + 2
                other = j - 1 if f % 2 == 0 else j + 1
                va[xf, :, part] = e0s[xf, :, part] + ok * (0.75 * cy0[j, t] + 0.25 * cy0[other, t])
    relax(va, vb, 2, 38, 9, k0[...], lambda p, q: fr0 * r0s[p:q], side0)
    relax(vb, va, 3, 37, 9, k0[...], lambda p, q: fr0 * r0s[p:q], side0)
    total = jnp.zeros((32, 128), F32)
    last = m0[:, :128]
    for p, q in chunks(4, 36, 8):
        mid = va[p:q]
        flat = va[p:q, :, :128]
        near = (va[p + 1 : q + 1, :, :128] + va[p - 1 : q - 1, :, :128]) + (
            pltpu.roll(flat, 1, 1) + pltpu.roll(flat, 39, 1)
        )
        value = (r0s[p:q, :, :128] - times(mid, last) + S0 * near)[:, 4:36]
        part = slice(p - 4, q - 4)
        res[part] = value
        sol[part] = va[p:q, 4:36, :128]
        total = total + jnp.sum(value * value, axis=0)
    sum3 = jnp.sum(total)
    tile = rows((1, 128), 1)
    stat[...] = jnp.where(
        tile == 0, stat0[0:1], jnp.where(tile == 1, stat1[0:1], jnp.where(tile == 2, sum2, jnp.where(tile == 3, sum3, 0.0)))
    )


def store_kernel(a, b, a_out, b_out, sems):
    sends = [pltpu.make_async_copy(x, y, sems.at[i]) for i, (x, y) in enumerate(((a, a_out), (b, b_out)))]
    for send in sends:
        send.start()
    for send in sends:
        send.wait()


def shift(x, axis, k):
    n = lax.axis_size(axis)
    return lax.ppermute(x, axis, [((i + k) % n, i) for i in range(n)])


def swap(x, axis, flip):
    return lax.ppermute(x, axis, [(i ^ flip, i) for i in range(lax.axis_size(axis))])


def f32(*shape):
    return pltpu.VMEM(shape, F32)


def bf16(*shape):
    return pltpu.VMEM(shape, BF16)


def scratch(*shape):
    return pltpu.VMEM(shape, F32)


def call(kernel, outs, scratches, name, limit=16, away=(), home=()):
    def run(*operands):
        operands = [x if i in home else pltpu.with_memory_space_constraint(x, pltpu.VMEM) for i, x in enumerate(operands)]
        return pl.pallas_call(
            kernel,
            out_shape=[jax.ShapeDtypeStruct(o.shape, F32) if i in away else o for i, o in enumerate(outs)],
            in_specs=[pl.BlockSpec(memory_space=pltpu.VMEM)] * len(operands),
            out_specs=[pl.BlockSpec(memory_space=pl.ANY if i in away else pltpu.VMEM) for i in range(len(outs))],
            scratch_shapes=scratches,
            compiler_params=pltpu.CompilerParams(vmem_limit_bytes=limit * 2**20),
            name=name,
        )(*operands)

    return run


def body(data, weights):
    own, to_left, to_right = call(
        prepare_kernel, [f32(32, 32, 128), f32(12, 32, 128), f32(12, 32, 128)], [], "prepare", home=(0, 1)
    )(data, weights)
    from_right, from_left = shift(to_left, "gz", 1), shift(to_right, "gz", -1)
    tail, first, last = call(
        spread_0_kernel, [f32(32, 32, 128), f32(5, 32, 128), f32(5, 32, 128)], [], "spread_0"
    )(own, from_right, from_left)
    xlo, xhi = shift(last, "gx", -1), shift(first, "gx", 1)
    low, high = call(edges_0_kernel, [f32(60, 4, 128), f32(60, 4, 128)], [], "edges_0")(own, tail, xlo, xhi)
    ylo, yhi = shift(high, "gy", -1), shift(low, "gy", 1)
    (field,) = call(gather_0_kernel, [f32(40, 40, 256)], [], "gather_0")(own, tail, xlo, xhi)
    b0, k0, m0, f0 = call(
        weights_0_kernel, [bf16(768, 256), bf16(768, 256), bf16(768, 256), f32(8, 256)], [], "weights_0"
    )(from_left, weights, from_right)
    k1, k1u, m1, f1 = call(
        weights_1_kernel, [bf16(768, 128), bf16(384, 128), bf16(384, 128), f32(8, 256)], [], "weights_1"
    )(from_left, weights, from_right)
    big = (40, 40, 256)
    r1, to_left, to_right, e0s, r0s, stat0 = call(
        down_0_kernel,
        [f32(16, 16, 128), f32(6, 16, 128), f32(6, 16, 128), f32(*big), f32(*big), f32(8, 128)],
        [scratch(*big), scratch(*big), scratch(*big), scratch(*big), scratch(16, 2, 40, 128)],
        "down_0",
    )(field, ylo, yhi, b0, k0, m0, f0)
    from_right, from_left = shift(to_left, "gz", 1), shift(to_right, "gz", -1)
    wide1, tail1, first, last = call(
        spread_1_kernel, [f32(16, 16, 128), f32(16, 16, 128), f32(6, 16, 128), f32(6, 16, 128)], [], "spread_1"
    )(r1, from_right, from_left)
    xlo, xhi = shift(last, "gx", -1), shift(first, "gx", 1)
    low, high = call(edges_1_kernel, [f32(26, 8, 128), f32(26, 8, 128)], [], "edges_1")(wide1, tail1, xlo, xhi)
    ylo, yhi = shift(high, "gy", -1), shift(low, "gy", 1)
    mid = (26, 32, 128)
    msg, e1s, r1s, stat1 = call(
        down_1_kernel,
        [f32(3, 8, 128), f32(*mid), f32(*mid), f32(8, 128)],
        [scratch(*mid), scratch(*mid), scratch(*mid), scratch(*mid), scratch(8, 32, 128)],
        "down_1",
    )(wide1, tail1, xlo, xhi, ylo, yhi, k1, m1, f1, weights)
    near = {k: shift(msg, "gz", k) for k in (1, -1, 2, -2, 3, -3)}
    r2z, wide2 = call(join_kernel, [f32(16, 8, 128), f32(8, 256)], [], "join")(
        msg, near[1], near[2], near[3], near[-3], near[-2], near[-1]
    )
    k2, k2u, m2, f2, k3, f3 = call(
        weights_2_kernel,
        [bf16(768, 256), bf16(384, 128), bf16(768, 256), f32(8, 256), bf16(384, 128), f32(8, 128)],
        [], "weights_coarse",
    )(wide2)
    x1, x2, x3 = shift(r2z, "gx", 1), shift(r2z[:8], "gx", 2), shift(r2z, "gx", 3)
    r2x, low, high = call(edges_2_kernel, [f32(50, 8, 128), f32(18, 3, 128), f32(18, 3, 128)], [], "edges_2")(
        r2z, x1, x2, x3
    )
    ya, yb = shift(r2x, "gy", -1), shift(r2x, "gy", 1)
    yc, yd = shift(high, "gy", -2), shift(low, "gy", 2)
    lev2 = (30, 32, 256)
    sol, res, stat = call(
        up_kernel,
        [f32(32, 32, 128), f32(32, 32, 128), f32(1, 128)],
        [
            scratch(*lev2), scratch(*lev2), scratch(*lev2), scratch(*lev2), scratch(12, 2, 40, 128),
            scratch(14, 32, 128), scratch(12, 16, 128), scratch(12, 16, 128), scratch(12, 16, 128),
            scratch(12, 32, 128), scratch(*mid), scratch(*mid), scratch(*mid), scratch(14, 32, 128),
            scratch(*big), scratch(*big), scratch(*big), scratch(20, 2, 40, 128),
        ],
        "up", 24,
    )(r2x, ya, yb, yc, yd, k2, k2u, m2, f2, k3, f3, k1u, f1, e1s, r1s, k0, m0, f0, e0s, r0s, stat0, stat1)
    sol, res = call(
        store_kernel, [f32(32, 32, 128), f32(32, 32, 128)], [pltpu.SemaphoreType.DMA((2,))], "store", 4, (0, 1)
    )(sol, res)
    t = stat
    for axis, flips in (("gy", (1,)), ("gx", (1, 2, 3)), ("gy", (2, 4, 6)), ("gz", (1, 2, 3)), ("gz", (7,))):
        others = [swap(t, axis, f) for f in flips]
        t = t + others[0]
        if len(others) > 1:
            t = t + (others[1] + others[2])
    cells = jnp.array([NX * NY * NZ >> (3 * k) for k in (0, 1, 2, 0)], F32)
    return sol, res, jnp.sqrt(t[0, :4] / cells)


def solution(mesh):
    placed = (P("gx", "gy", "gz"), P(None, "gz"))
    return jax.shard_map(
        body,
        mesh=mesh,
        in_specs=placed,
        out_specs=(P("gx", "gy", "gz"), P("gx", "gy", "gz"), P()),
        check_vma=False,
    )
```

```python
import jax
import jax.numpy as jnp
from jax import lax
from jax.sharding import PartitionSpec as P
from jax.experimental import pallas as pl
from jax.experimental.pallas import tpu as pltpu

OFFSETS = (-4, -3, -2, -1, 1, 2, 3, 4)
RELAX = 0.45
NX, NY, NZ = 128, 256, 1024
F32, BF16 = jnp.float32, jnp.bfloat16
H0, H1, H2, H3 = 4, 5, 11, 4
S0, S1, S2, S3 = 1.0, 0.25, 0.0625, 0.015625
SLOT = 40
TAILS = {1: (0, 28), 2: (56, 20), 3: (96, 12), 4: (120, 4)}


def place_0(p):
    return jnp.where(p < 192, p, p - 256)


def place_1(p):
    lane = p & 127
    return jnp.where((lane < 96) == (p < 128), lane, lane - 128)


def place_2(p):
    lane = p & 127
    return jnp.where((lane < 80) == (p < 128), lane, lane - 128)


def place_3(p):
    return jnp.where(p < 64, p, p - 128)


def inside(z, iz, level, reach):
    count = 128 >> level
    glob = iz * count + z
    return (z >= -reach) & (z < count + reach) & (glob >= 0) & (glob < (NZ >> level))


def rows(shape, dim):
    return lax.broadcasted_iota(jnp.int32, shape, dim)


def halves(a):
    hi = a.astype(BF16)
    return hi, (a - hi.astype(F32)).astype(BF16)


def thrice(matrix):
    hi, lo = halves(matrix)
    return jnp.concatenate([hi, hi, lo], axis=0)


def times(field, matrix):
    shape = field.shape
    hi, lo = halves(field.reshape(shape[0] * shape[1], shape[2]))
    out = jnp.dot(jnp.concatenate([hi, lo, hi], axis=1), matrix, preferred_element_type=F32)
    return out.reshape(shape[0], shape[1], matrix.shape[1])


def times_exact(field, matrix):
    shape = field.shape
    hi, lo = halves(field.reshape(shape[0] * shape[1], shape[2]))
    out = jnp.dot(jnp.concatenate([hi, lo], axis=1), matrix, preferred_element_type=F32)
    return out.reshape(shape[0], shape[1], matrix.shape[1])


def exact(a, b):
    return jnp.dot(a, b, precision=lax.Precision.HIGHEST, preferred_element_type=F32)


def operators(w, place, iz, level, reach, stiffness):
    n = w.shape[1]
    zk = place(rows((n, n), 0))
    zn = place(rows((n, n), 1))
    both = inside(zk, iz, level, reach) & inside(zn, iz, level, reach)
    gap = jnp.where(both, zk - zn, 99)
    band = jnp.where(gap == 0, 1.0, 0.0)
    eye = jnp.where(rows((n, n), 0) == rows((n, n), 1), 1.0, 0.0)
    for j, offset in enumerate(OFFSETS):
        band = jnp.where(gap == offset, w[j : j + 1, :], band)
    gram = lax.dot_general(
        band, band, (((1,), (1,)), ((), ())), precision=lax.Precision.HIGHEST, preferred_element_type=F32
    )
    diag = jnp.sum(gram * eye, axis=0, keepdims=True) + 6.0 * stiffness
    line = inside(place(rows((1, n), 1)), iz, level, reach)
    factor = jnp.where(line, RELAX / diag, 0.0)
    op = gram + stiffness * (6.0 * eye - jnp.where((gap == 1) | (gap == -1), 1.0, 0.0))
    return band, op, eye - op * factor, factor


def restrict_matrix(place_f, n_f, place_c, n_c, iz, level, reach):
    zf = place_f(rows((n_f, n_c), 0))
    zc = place_c(rows((n_f, n_c), 1))
    gap = zf - 2 * zc
    near = jnp.where((gap == 0) | (gap == 1), 0.375, 0.0) + jnp.where((gap == -1) | (gap == 2), 0.125, 0.0)
    m = jnp.where(inside(zf, iz, level, reach), near, 0.0).astype(BF16)
    return jnp.concatenate([m, m], axis=0)


def prolong_matrix(place_c, n_c, place_f, n_f, iz, level, reach):
    zc = place_c(rows((n_c, n_f), 0))
    zf = place_f(rows((n_c, n_f), 1))
    gap = zf - 2 * zc
    near = jnp.where((gap == 0) | (gap == 1), 0.75, 0.0) + jnp.where((gap == -1) | (gap == 2), 0.25, 0.0)
    m = jnp.where(inside(zf, iz, level, reach), near, 0.0).astype(BF16)
    return jnp.concatenate([m, m], axis=0)


def plane_mask(shape, level, ix, iy, reach):
    x = ix * (32 >> level) + rows(shape, 0) - reach
    y = iy * (32 >> level) + rows(shape, 1) - reach
    ok = (x >= 0) & (x < (NX >> level)) & (y >= 0) & (y < (NY >> level))
    return jnp.where(ok, 1.0, 0.0)


def around(ref, a, b):
    mid = ref[a:b]
    count = mid.shape[1]
    return mid, (ref[a + 1 : b + 1] + ref[a - 1 : b - 1]) + (pltpu.roll(mid, 1, 1) + pltpu.roll(mid, count - 1, 1))


def chunks(a, b):
    mid = (a + b + 1) // 2
    return [(a, mid), (mid, b)]


def relax(src, dst, a, b, matrix, right, side):
    for p, q in chunks(a, b):
        mid, near = around(src, p, q)
        dst[p:q] = times(mid, matrix) + right(p, q) + side[p:q] * near


def pack_lanes(planes, height, width, count, to_left, to_right):
    lane = rows((height, 128), 1)
    for g in range(-(-len(planes) // 3)):
        left, right = None, None
        for i, value in enumerate(planes[3 * g : 3 * g + 3]):
            a = pltpu.roll(value, SLOT * i, 1) if i else value
            b = pltpu.roll(value, (SLOT * i + width - count) % 128, 1)
            left = a if i == 0 else jnp.where(lane < SLOT * i, left, a)
            right = b if i == 0 else jnp.where(lane < SLOT * i, right, b)
        to_left[g] = left
        to_right[g] = right


def prepare_kernel(data, weights, own, w, to_left, to_right, sems):
    copies = [
        pltpu.make_async_copy(data.at[pl.ds(8 * g, 8)], own.at[pl.ds(8 * g, 8)], sems.at[g]) for g in range(4)
    ]
    copies.append(pltpu.make_async_copy(weights, w, sems.at[4]))
    for copy in copies:
        copy.start()
    lane = rows((32, 128), 1)
    thin = [jnp.zeros((32, 128), F32)] * 2
    for g in range(8):
        if g % 2 == 0:
            copies[g // 2].wait()
        left, right = own[4 * g], None
        for i in range(4):
            p = 4 * g + i
            value = own[p]
            if i:
                left = jnp.where(lane < 32 * i, left, pltpu.roll(value, 32 * i, 1))
            b = pltpu.roll(value, 32 * i + 32, 1) if i < 3 else value
            right = b if i == 0 else jnp.where(lane < 32 * i, right, b)
            here = (lane >= 4 * p) & (lane < 4 * p + 4)
            thin[0] = jnp.where(here, pltpu.roll(value, (4 * p - 32) % 128, 1) if p != 8 else value, thin[0])
            thin[1] = jnp.where(here, pltpu.roll(value, (4 * p - 92) % 128, 1) if p != 23 else value, thin[1])
        to_left[32 * g : 32 * g + 32] = left
        to_right[32 * g : 32 * g + 32] = right
    to_left[256:288] = thin[0]
    to_right[256:288] = thin[1]
    copies[4].wait()
    to_left[288:296] = w[...]
    to_right[288:296] = w[...]


def turned(value, amount):
    return pltpu.roll(value, amount % 128, 1) if amount % 128 else value


def spread_0_kernel(own, from_right, from_left, tail, first, last):
    lane = rows((32, 128), 1)
    packed = [jnp.zeros((32, 128), F32)] * 2
    thin_right, thin_left = from_right[256:288], from_left[256:288]
    for p in range(32):
        g, i = divmod(p, 4)
        right = turned(from_right[32 * g : 32 * g + 32], -32 * i)
        left = turned(from_left[32 * g : 32 * g + 32], 96 - 32 * i)
        right = jnp.where(lane < 32, right, turned(thin_right, 32 - 4 * p))
        left = jnp.where(lane < 96, turned(thin_left, 92 - 4 * p), left)
        value = jnp.where(lane < 36, right, jnp.where(lane >= 92, left, 0.0))
        tail[p] = value
        for side, far in ((0, p + 1), (1, 32 - p)):
            if far <= H0:
                begin, reach = TAILS[far]
                moved = pltpu.roll(value, begin + reach, 1)
                packed[side] = jnp.where((lane >= begin) & (lane < begin + 2 * reach), moved, packed[side])
    first[:H0] = own[:H0]
    first[H0] = packed[0]
    last[:H0] = own[32 - H0 :]
    last[H0] = packed[1]


def edges_0_kernel(own, tail, xlo, xhi, low, high):
    lane = rows((4, 128), 1)

    def ends(ref, p):
        value = ref[p]
        return value[:H0], value[32 - H0 :]

    def tails(p):
        if H0 <= p < 32 + H0:
            return ends(tail, p - H0)
        source = xlo if p < H0 else xhi
        begin, reach = TAILS[H0 - p if p < H0 else p - 31 - H0]
        out = []
        for value in ends(source, H0):
            moved = pltpu.roll(value, (128 - begin - reach) % 128, 1)
            out.append(jnp.where((lane < reach) | (lane >= 128 - reach), moved, 0.0))
        return out

    kept = None
    for p in range(40):
        if p < H0:
            a, b = ends(xlo, p)
        elif p < 32 + H0:
            a, b = ends(own, p - H0)
        else:
            a, b = ends(xhi, p - 32 - H0)
        low[p] = a
        high[p] = b
        moved = [pltpu.roll(v, 28 if p % 2 == 0 else 92, 1) for v in tails(p)]
        if p % 2 == 0:
            kept = moved
        else:
            low[40 + p // 2] = jnp.where(lane < 64, kept[0], moved[0])
            high[40 + p // 2] = jnp.where(lane < 64, kept[1], moved[1])


def gather_0_kernel(own, tail, xlo, xhi, field):
    ix = lax.axis_index("gx")
    lane = rows((32, 128), 1)
    for p in range(40):
        if H0 <= p < 32 + H0:
            field[p, 4:36, :128] = own[p - H0]
            field[p, 4:36, 128:] = tail[p - H0]
        else:
            source, q = (xlo, p) if p < H0 else (xhi, p - 32 - H0)
            begin, reach = TAILS[H0 - p if p < H0 else p - 31 - H0]
            xr = ix * 32 + p - H0
            ok = jnp.where((xr >= 0) & (xr < NX), 1.0, 0.0)
            moved = pltpu.roll(source[H0], (128 - begin - reach) % 128, 1)
            field[p, 4:36, :128] = source[q] * ok
            field[p, 4:36, 128:] = jnp.where((lane < reach) | (lane >= 128 - reach), moved, 0.0) * ok
        field[p, :4] = jnp.zeros((4, 256), F32)
        field[p, 36:] = jnp.zeros((4, 256), F32)


def weights_0_kernel(left, own, right, b0, k0, m0, f0, fold, grow, side):
    ix, iy, iz = lax.axis_index("gx"), lax.axis_index("gy"), lax.axis_index("gz")
    lane = rows((8, 128), 1)
    laid = jnp.concatenate([own[...], jnp.where(lane < 64, right[288:296], left[288:296])], axis=1)
    band, op, step, factor = operators(laid, place_0, iz, 0, 36, S0)
    b0[...] = thrice(jnp.transpose(band))
    k0[...] = thrice(step)
    m0[...] = thrice(op)
    f0[...] = jnp.broadcast_to(factor, (8, 256))
    fold[...] = restrict_matrix(place_0, 256, lambda q: q, 128, iz, 0, 36)
    grow[...] = prolong_matrix(place_1, 128, place_0, 256, iz, 0, 36)
    y = iy * 32 + rows((40, 256), 0) - H0
    column = jnp.where((y >= 0) & (y < NY), factor * S0, 0.0)
    for p in range(40):
        xr = ix * 32 + p - H0
        side[p] = column * jnp.where((xr >= 0) & (xr < NX), 1.0, 0.0)


def weights_1_kernel(left, own, right, k1, k1u, m1, f1, fold, grow, side):
    ix, iy, iz = lax.axis_index("gx"), lax.axis_index("gy"), lax.axis_index("gz")
    wide = jnp.concatenate([left[288:296], own[...], right[288:296]], axis=1)
    mean = jnp.where((rows((384, 256), 0) - 128) >> 1 == place_1(rows((384, 256), 1)), 0.5, 0.0)
    band, op, step, factor = operators(exact(wide, mean), place_1, iz, 1, 41, S1)
    k1[...] = thrice(step[:, :128])
    k1u[...] = thrice(step[:128, :128])
    m1[...] = thrice(op[:128, :128])
    f1[...] = jnp.broadcast_to(factor, (8, 256))
    fold[...] = restrict_matrix(place_1, 128, lambda q: q, 128, iz, 1, 32)
    grow[...] = prolong_matrix(place_2, 128, place_1, 128, iz, 1, 41)
    yrow = rows((32, 128), 0)
    y = iy * 16 + yrow - H1
    column = jnp.where((y >= 0) & (y < NY // 2) & (yrow < 26), factor[:, :128] * S1, 0.0)
    for p in range(26):
        xr = ix * 16 + p - H1
        side[p] = column * jnp.where((xr >= 0) & (xr < NX // 2), 1.0, 0.0)


def spread_1_kernel(own, from_right, from_left, main, rest, first, last):
    lane = rows((16, 128), 1)
    for p in range(16):
        group, i = divmod(p, 3)
        right = pltpu.roll(from_right[group], (64 - SLOT * i) % 128, 1)
        left = pltpu.roll(from_left[group], (91 - SLOT * i) % 128, 1)
        one = jnp.where(lane < 64, own[p], jnp.where(lane < 101, right, 0.0))
        two = jnp.where(lane >= 91, left, 0.0)
        main[p] = jnp.where(lane < 96, one, two)
        rest[p] = jnp.where(lane < 96, two, one)
    first[:H1] = main[:H1]
    first[H1] = rest[0]
    last[:H1] = main[16 - H1 :]
    last[H1] = rest[15]


def edges_1_kernel(main, rest, xlo, xhi, low, high):
    for p in range(26):
        if p < H1:
            value, tail = xlo[p], xlo[H1] if p == H1 - 1 else None
        elif p < 16 + H1:
            value, tail = main[p - H1], rest[p - H1]
        else:
            value, tail = xhi[p - 16 - H1], xhi[H1] if p == 16 + H1 else None
        low[p, :H1] = value[:H1]
        high[p, :H1] = value[16 - H1 :]
        none = jnp.zeros((8 - H1, 128), F32)
        low[p, H1:] = none
        high[p, H1:] = none
        if tail is not None:
            low[p, H1 : H1 + 1] = tail[0:1]
            high[p, H1 : H1 + 1] = tail[15:16]


def down_0_kernel(
    field, ylo, yhi, b0, k0, m0, f0, fold, side, r1, to_left, to_right, e_out, r_out, stat, d, e0, g, gx
):
    ix, iy, iz = lax.axis_index("gx"), lax.axis_index("gy"), lax.axis_index("gz")
    low_ok = jnp.where(iy > 0, 1.0, 0.0)
    high_ok = jnp.where(iy < 7, 1.0, 0.0)
    lane = rows((4, 128), 1)
    for p in range(40):
        xr = ix * 32 + p - H0
        ok = jnp.where((xr >= 0) & (xr < NX), 1.0, 0.0)
        d[p, 4:36] = field[p, 4:36]
        for edge, part, good in ((ylo, slice(0, 4), low_ok), (yhi, slice(36, 40), high_ok)):
            moved = pltpu.roll(edge[40 + p // 2], 100 if p % 2 == 0 else 36, 1)
            d[p, part, :128] = edge[p] * (ok * good)
            d[p, part, 128:] = jnp.where((lane < 28) | (lane >= 100), moved, 0.0) * (ok * good)
    factor = f0[0:1, :].reshape(1, 1, 256)
    for p, q in chunks(0, 40):
        r = times(d[p:q], b0[...])
        r_out[p:q] = r
        e0[p:q] = r * factor
    relax(e0, e_out, 1, 39, k0[...], lambda p, q: e0[p:q], side)
    e_out[0] = jnp.zeros((40, 256), F32)
    e_out[39] = jnp.zeros((40, 256), F32)
    total = jnp.zeros((40, 128), F32)
    for p, q in chunks(3, 37):
        mid, near = around(e_out, p, q)
        value = r_out[p:q] - times(mid, m0[...]) + S0 * near
        x = ix * 32 + rows(value.shape, 0) + (p - H0)
        y = iy * 32 + rows(value.shape, 1) - H0
        value = jnp.where((x >= 0) & (x < NX) & (y >= 0) & (y < NY), value, 0.0)
        g[p:q] = value
        own = value[max(p, 4) - p : min(q, 36) - p, :, :128]
        total = total + jnp.sum(own * own, axis=0)
    row = rows((40, 128), 0)
    stat[...] = jnp.full((8, 128), jnp.sum(jnp.where((row >= 4) & (row < 36), total, 0.0)), F32)
    for i in range(16):
        value = ((g[2 * i + 3] + g[2 * i + 6]) + 3.0 * (g[2 * i + 4] + g[2 * i + 5])) * 0.125
        gx[i, 0] = value[:, :128]
        gx[i, 1] = value[:, 128:]
    gy = [
        jnp.concatenate([gx[:, t, pl.ds(3 + a, 16, stride=2), :] for t in range(2)], axis=2) for a in range(4)
    ]
    gy = ((gy[0] + gy[3]) + 3.0 * (gy[1] + gy[2])) * 0.125
    out = times_exact(gy, fold[...])
    r1[...] = out
    pack_lanes([out[i] for i in range(16)], 16, 37, 64, to_left, to_right)


def down_1_kernel(wide, tail, xlo, xhi, ylo, yhi, k1, m1, f1, fold, side, w, msg, e_out, r_out, stat, e0, e0b, g, gx):
    ix, iy, iz = lax.axis_index("gx"), lax.axis_index("gy"), lax.axis_index("gz")
    lane = rows((32, 128), 1)
    yrow = rows((32, 128), 0)
    y = iy * 16 + yrow - H1
    inner = jnp.where((y >= 0) & (y < NY // 2) & (yrow < 26), 1.0, 0.0)
    for p in range(26):
        xr = ix * 16 + p - H1
        ok = inner * jnp.where((xr >= 0) & (xr < NX // 2), 1.0, 0.0)
        if p < H1:
            value, extra = xlo[p], xlo[H1] if p == H1 - 1 else jnp.zeros((16, 128), F32)
        elif p < 16 + H1:
            value, extra = wide[p - H1], tail[p - H1]
        else:
            value, extra = xhi[p - 16 - H1], xhi[H1] if p == 16 + H1 else jnp.zeros((16, 128), F32)
        main = jnp.concatenate([ylo[p, :H1], value, yhi[p, :H1], jnp.zeros((6, 128), F32)], axis=0) * ok
        rest = jnp.concatenate(
            [jnp.zeros((4, 128), F32), ylo[p, H1 : H1 + 1], extra, yhi[p, H1 : H1 + 1], jnp.zeros((10, 128), F32)],
            axis=0,
        ) * ok
        r_out[p] = main
        e0[p] = main * f1[0:1, :128]
        e0b[p] = rest * f1[0:1, 128:]
    for p, q in chunks(1, 25):
        mid, near = around(e0, p, q)
        both = jnp.concatenate([mid, e0b[p:q]], axis=2)
        e_out[p:q] = times(both, k1[...]) + mid + side[p:q] * near
    e_out[0] = jnp.zeros((32, 128), F32)
    e_out[25] = jnp.zeros((32, 128), F32)
    total = jnp.zeros((32, 128), F32)
    for p, q in chunks(4, 22):
        mid, near = around(e_out, p, q)
        value = r_out[p:q] - times(mid, m1[...]) + S1 * near
        x = ix * 16 + rows(value.shape, 0) + (p - H1)
        y = iy * 16 + rows(value.shape, 1) - H1
        value = jnp.where((x >= 0) & (x < NX // 2) & (y >= 0) & (y < NY // 2), value, 0.0)
        g[p:q] = value
        own = value[max(p, 5) - p : min(q, 21) - p]
        total = total + jnp.sum(own * own, axis=0)
    row = rows((32, 128), 0)
    keep = (row >= 5) & (row < 21) & (lane < 64)
    stat[...] = jnp.full((8, 128), jnp.sum(jnp.where(keep, total, 0.0)), F32)
    for i in range(8):
        gx[i] = ((g[2 * i + 4] + g[2 * i + 7]) + 3.0 * (g[2 * i + 5] + g[2 * i + 6])) * 0.125
    gy = [gx[:, pl.ds(4 + a, 8, stride=2), :] for a in range(4)]
    gy = ((gy[0] + gy[3]) + 3.0 * (gy[1] + gy[2])) * 0.125
    out = times_exact(gy, fold[...])[:, :, :32]
    for k in range(2):
        msg[k] = jnp.concatenate([out[4 * k + i] for i in range(4)], axis=1)
    mean = jnp.where(rows((128, 128), 0) >> 2 == rows((128, 128), 1), 0.25, 0.0)
    msg[2] = exact(w[...], mean)


def join_kernel(own, r1, r2, r3, l3, l2, l1, both, w):
    lane = rows((8, 128), 1)
    blocks = (own, r1, r2, r3), (None, l3, l2, l1)
    for p in range(9):
        k, i = divmod(p, 4)
        part = slice(32 * i, 32 * i + 32)
        first, second = (
            jnp.concatenate([jnp.zeros((8, 32), F32) if b is None else b[k, :, part] for b in group], axis=1)
            for group in blocks
        )
        main, rest = jnp.where(lane < 80, first, second), jnp.where(lane < 80, second, first)
        if p < 8:
            both[p] = main
            both[8 + p] = rest
        else:
            w[:, :128] = main
            w[:, 128:] = rest


def edges_2_kernel(own, x1, x2, x3, near, low, high):
    near[:3] = x2[5:]
    near[3:11] = x3[:8]
    near[11:19] = own[:8]
    near[19:27] = x1[:8]
    near[27:30] = x2[:3]
    near[30:36] = x3[10:]
    near[36:44] = own[8:]
    near[44:50] = x1[8:14]
    for i in range(18):
        value = near[i + 6]
        low[i] = value[:3]
        high[i] = value[5:]


def weights_2_kernel(w2, k2, k2u, m2, f2, k3, f3, fold, grow, side):
    ix, iy, iz = lax.axis_index("gx"), lax.axis_index("gy"), lax.axis_index("gz")
    band, op, step, factor = operators(w2[...], place_2, iz, 2, 69, S2)
    k2[...] = thrice(step)
    k2u[...] = thrice(step[:128, :128])
    m2[...] = thrice(op)
    f2[...] = jnp.broadcast_to(factor, (8, 256))
    fold[...] = restrict_matrix(place_2, 256, place_3, 128, iz, 2, 65)
    grow[...] = prolong_matrix(place_3, 128, place_2, 128, iz, 2, 69)
    yrow = rows((32, 256), 0)
    y = iy * 8 + yrow - H2
    column = jnp.where((y >= 0) & (y < NY // 4) & (yrow < 30), factor * S2, 0.0)
    for p in range(30):
        xr = ix * 8 + p - H2
        side[p] = column * jnp.where((xr >= 0) & (xr < NX // 4), 1.0, 0.0)
    mean = jnp.where(place_2(rows((256, 128), 0)) >> 1 == place_3(rows((256, 128), 1)), 0.5, 0.0)
    band, op, step, factor = operators(exact(w2[...], mean), place_3, iz, 3, 28, S3)
    k3[...] = thrice(step)
    f3[...] = jnp.broadcast_to(factor, (8, 128))


def up_kernel(
    r2x, ya, yb, yc, yd, k2, k2u, m2, f2, k3, f3, fold2, grow2, side2,
    k1, f1, e1s, r1s, grow1, side1, k0, m0, f0, e0s, r0s, grow0, side0, stat0, stat1,
    sol, res, stat,
    ra, ea, eb, gx2, r3, e3, side3, c3, cy2, ua, ub, cy1, va, vb, cy0,
):
    ix, iy, iz = lax.axis_index("gx"), lax.axis_index("gy"), lax.axis_index("gz")
    lane = rows((32, 128), 1)
    yrow = rows((32, 128), 0)
    for p in range(30):
        xr = ix * 8 + p - H2
        y = iy * 8 + yrow - H2
        ok = jnp.where(
            (y >= 0) & (y < NY // 4) & (yrow < 30), jnp.where((xr >= 0) & (xr < NX // 4), 1.0, 0.0), 0.0
        )
        three, two = jnp.zeros((3, 128), F32), jnp.zeros((2, 128), F32)
        far = 6 <= p < 24
        main = jnp.concatenate(
            [yc[p - 6] if far else three, ya[p], r2x[p], yb[p], yd[p - 6] if far else three, two], axis=0
        ) * ok
        rest = jnp.zeros((32, 128), F32)
        if 5 <= p < 25:
            rest = jnp.concatenate([three, ya[p + 25], r2x[p + 25], yb[p + 25], three, two], axis=0) * ok
        ra[p, :, :128] = main
        ra[p, :, 128:] = rest
        ea[p, :, :128] = main * f2[0:1, :128]
        ea[p, :, 128:] = rest * f2[0:1, 128:]
    relax(ea, eb, 1, 29, k2[...], lambda p, q: ea[p:q], side2)
    total = jnp.zeros((32, 128), F32)
    for p, q in chunks(2, 28):
        mid, near = around(eb, p, q)
        value = ra[p:q] - times(mid, m2[...]) + S2 * near
        x = ix * 8 + rows(value.shape, 0) + (p - H2)
        y = iy * 8 + rows(value.shape, 1) - H2
        value = jnp.where((x >= 0) & (x < NX // 4) & (y >= 0) & (y < NY // 4), value, 0.0)
        ea[p:q] = value
        own = value[max(p, 11) - p : min(q, 19) - p, :, :128]
        total = total + jnp.sum(own * own, axis=0)
    keep = (yrow >= 11) & (yrow < 19) & (lane < 32)
    sum2 = jnp.sum(jnp.where(keep, total, 0.0))
    for i in range(12):
        value = ((ea[2 * i + 2] + ea[2 * i + 5]) + 3.0 * (ea[2 * i + 3] + ea[2 * i + 4])) * 0.125
        gx2[i, 0, :32] = value[:, :128]
        gx2[i, 1, :32] = value[:, 128:]
        gx2[i, 0, 32:] = jnp.zeros((8, 128), F32)
        gx2[i, 1, 32:] = jnp.zeros((8, 128), F32)
    gy = [
        jnp.concatenate([gx2[:, t, pl.ds(2 + a, 16, stride=2), :] for t in range(2)], axis=2) for a in range(4)
    ]
    gy = ((gy[0] + gy[3]) + 3.0 * (gy[1] + gy[2])) * 0.125
    mask = plane_mask((12, 16, 128), 3, ix, iy, H3)
    right3 = times_exact(gy, fold2[...]) * mask
    factor3 = f3[0:1, :].reshape(1, 1, 128)
    e3[...] = right3 * factor3
    side3[...] = mask * (factor3 * S3)
    c3[...] = jnp.zeros((12, 16, 128), F32)
    relax(e3, c3, 1, 11, k3[...], lambda p, q: e3[p:q], side3)
    cz = times_exact(c3[...], grow2[...])
    below, above = pltpu.roll(cz, 1, 1), pltpu.roll(cz, 15, 1)
    cy2[...] = jnp.zeros((12, 32, 128), F32)
    cy2[:, pl.ds(3, 12, stride=2), :] = (0.75 * cz + 0.25 * below)[:, :12]
    cy2[:, pl.ds(4, 12, stride=2), :] = (0.75 * cz + 0.25 * above)[:, :12]
    fr2 = f2[0:1, :128].reshape(1, 1, 128)
    for xf in range(6, 24):
        f = xf - H2
        j = f // 2 + 4
        other = j - 1 if f % 2 == 0 else j + 1
        xr = ix * 8 + f
        y = iy * 8 + yrow - H2
        ok = jnp.where((y >= 0) & (y < NY // 4), jnp.where((xr >= 0) & (xr < NX // 4), 1.0, 0.0), 0.0)
        ea[xf, :, :128] = eb[xf, :, :128] + ok * (0.75 * cy2[j] + 0.25 * cy2[other])

    def relax_2(src, dst, a, b):
        for p, q in chunks(a, b):
            mid = src[p:q, :, :128]
            near = (src[p + 1 : q + 1, :, :128] + src[p - 1 : q - 1, :, :128]) + (
                pltpu.roll(mid, 1, 1) + pltpu.roll(mid, 31, 1)
            )
            dst[p:q, :, :128] = times(mid, k2u[...]) + fr2 * ra[p:q, :, :128] + side2[p:q, :, :128] * near

    relax_2(ea, eb, 7, 23)
    relax_2(eb, ea, 8, 22)
    for p in range(14):
        r3[p] = ea[8 + p, :, :128]
    r3[...] = times_exact(r3[...], grow1[...])
    cy1[...] = jnp.zeros((14, 32, 128), F32)
    cy1[:, pl.ds(1, 12, stride=2), :] = 0.75 * r3[:, 9:21, :] + 0.25 * r3[:, 8:20, :]
    cy1[:, pl.ds(2, 12, stride=2), :] = 0.75 * r3[:, 9:21, :] + 0.25 * r3[:, 10:22, :]
    fr1 = f1[0:1, :128].reshape(1, 1, 128)
    for xf in range(1, 25):
        f = xf - H1
        xr = ix * 16 + f
        y = iy * 16 + yrow - H1
        ok = jnp.where((y >= 0) & (y < NY // 2), jnp.where((xr >= 0) & (xr < NX // 2), 1.0, 0.0), 0.0)
        j = f // 2 + 3
        other = j - 1 if f % 2 == 0 else j + 1
        ua[xf] = e1s[xf] + ok * (0.75 * cy1[j] + 0.25 * cy1[other])
    relax(ua, ub, 2, 24, k1[...], lambda p, q: fr1 * r1s[p:q], side1)
    relax(ub, ua, 3, 23, k1[...], lambda p, q: fr1 * r1s[p:q], side1)
    for p, q in chunks(0, 20):
        cz = times_exact(ua[3 + p : 3 + q], grow0[...])
        for t in range(2):
            part = cz[:, :, 128 * t : 128 * t + 128]
            cy0[p:q, t, pl.ds(0, 20, stride=2), :] = 0.75 * part[:, 3:23] + 0.25 * part[:, 2:22]
            cy0[p:q, t, pl.ds(1, 20, stride=2), :] = 0.75 * part[:, 3:23] + 0.25 * part[:, 4:24]
    fr0 = f0[0:1, :].reshape(1, 1, 256)
    for xf in range(1, 39):
        f = xf - H0
        xr = ix * 32 + f
        y = iy * 32 + rows((40, 128), 0) - H0
        ok = jnp.where((y >= 0) & (y < NY), jnp.where((xr >= 0) & (xr < NX), 1.0, 0.0), 0.0)
        for t in range(2):
            part = slice(128 * t, 128 * t + 128)
            j = f // 2 + 2
            other = j - 1 if f % 2 == 0 else j + 1
            va[xf, :, part] = e0s[xf, :, part] + ok * (0.75 * cy0[j, t] + 0.25 * cy0[other, t])
    relax(va, vb, 2, 38, k0[...], lambda p, q: fr0 * r0s[p:q], side0)
    relax(vb, va, 3, 37, k0[...], lambda p, q: fr0 * r0s[p:q], side0)
    total = jnp.zeros((32, 128), F32)
    last = m0[:, :128]
    for p, q in chunks(4, 36):
        mid = va[p:q]
        flat = va[p:q, :, :128]
        near = (va[p + 1 : q + 1, :, :128] + va[p - 1 : q - 1, :, :128]) + (
            pltpu.roll(flat, 1, 1) + pltpu.roll(flat, 39, 1)
        )
        value = (r0s[p:q, :, :128] - times(mid, last) + S0 * near)[:, 4:36]
        part = slice(p - 4, q - 4)
        res[part] = value
        sol[part] = va[p:q, 4:36, :128]
        total = total + jnp.sum(value * value, axis=0)
    sum3 = jnp.sum(total)
    tile = rows((1, 128), 1)
    stat[...] = jnp.where(
        tile == 0, stat0[0:1], jnp.where(tile == 1, stat1[0:1], jnp.where(tile == 2, sum2, jnp.where(tile == 3, sum3, 0.0)))
    )


def store_kernel(a, b, a_out, b_out, sems):
    sends = [pltpu.make_async_copy(x, y, sems.at[i]) for i, (x, y) in enumerate(((a, a_out), (b, b_out)))]
    for send in sends:
        send.start()
    for send in sends:
        send.wait()


def shift(x, axis, k):
    n = lax.axis_size(axis)
    return lax.ppermute(x, axis, [((i + k) % n, i) for i in range(n)])


def swap(x, axis, flip):
    return lax.ppermute(x, axis, [(i ^ flip, i) for i in range(lax.axis_size(axis))])


def f32(*shape):
    return pltpu.VMEM(shape, F32)


def bf16(*shape):
    return pltpu.VMEM(shape, BF16)


def scratch(*shape):
    return pltpu.VMEM(shape, F32)


def call(kernel, outs, scratches, name, limit=16, away=(), home=()):
    def run(*operands):
        operands = [
            pltpu.with_memory_space_constraint(x, pltpu.HBM if i in home else pltpu.VMEM)
            for i, x in enumerate(operands)
        ]
        return pl.pallas_call(
            kernel,
            out_shape=[jax.ShapeDtypeStruct(o.shape, F32) if i in away else o for i, o in enumerate(outs)],
            in_specs=[pl.BlockSpec(memory_space=pltpu.HBM if i in home else pltpu.VMEM) for i in range(len(operands))],
            out_specs=[pl.BlockSpec(memory_space=pl.ANY if i in away else pltpu.VMEM) for i in range(len(outs))],
            scratch_shapes=scratches,
            compiler_params=pltpu.CompilerParams(vmem_limit_bytes=limit * 2**20),
            name=name,
        )(*operands)

    return run


def body(data, weights):
    own, w, to_left, to_right = call(
        prepare_kernel,
        [f32(32, 32, 128), f32(8, 128), f32(296, 128), f32(296, 128)],
        [pltpu.SemaphoreType.DMA((5,))], "prepare", home=(0, 1),
    )(data, weights)
    from_right, from_left = shift(to_left, "gz", 1), shift(to_right, "gz", -1)
    tail, first, last = call(
        spread_0_kernel, [f32(32, 32, 128), f32(5, 32, 128), f32(5, 32, 128)], [], "spread_0"
    )(own, from_right, from_left)
    xlo, xhi = shift(last, "gx", -1), shift(first, "gx", 1)
    low, high = call(edges_0_kernel, [f32(60, 4, 128), f32(60, 4, 128)], [], "edges_0")(own, tail, xlo, xhi)
    ylo, yhi = shift(high, "gy", -1), shift(low, "gy", 1)
    (field,) = call(gather_0_kernel, [f32(40, 40, 256)], [], "gather_0")(own, tail, xlo, xhi)
    b0, k0, m0, f0, r00, p00, side0 = call(
        weights_0_kernel,
        [
            bf16(768, 256), bf16(768, 256), bf16(768, 256), f32(8, 256), bf16(512, 128), bf16(256, 256),
            f32(40, 40, 256),
        ],
        [], "weights_0",
    )(from_left, w, from_right)
    k1, k1u, m1, f1, r01, p01, side1 = call(
        weights_1_kernel,
        [
            bf16(768, 128), bf16(384, 128), bf16(384, 128), f32(8, 256), bf16(256, 128), bf16(256, 128),
            f32(26, 32, 128),
        ],
        [], "weights_1",
    )(from_left, w, from_right)
    big = (40, 40, 256)
    r1, to_left, to_right, e0s, r0s, stat0 = call(
        down_0_kernel,
        [f32(16, 16, 128), f32(6, 16, 128), f32(6, 16, 128), f32(*big), f32(*big), f32(8, 128)],
        [scratch(*big), scratch(*big), scratch(*big), scratch(16, 2, 40, 128)],
        "down_0",
    )(field, ylo, yhi, b0, k0, m0, f0, r00, side0)
    from_right, from_left = shift(to_left, "gz", 1), shift(to_right, "gz", -1)
    wide1, tail1, first, last = call(
        spread_1_kernel, [f32(16, 16, 128), f32(16, 16, 128), f32(6, 16, 128), f32(6, 16, 128)], [], "spread_1"
    )(r1, from_right, from_left)
    xlo, xhi = shift(last, "gx", -1), shift(first, "gx", 1)
    low, high = call(edges_1_kernel, [f32(26, 8, 128), f32(26, 8, 128)], [], "edges_1")(wide1, tail1, xlo, xhi)
    ylo, yhi = shift(high, "gy", -1), shift(low, "gy", 1)
    mid = (26, 32, 128)
    msg, e1s, r1s, stat1 = call(
        down_1_kernel,
        [f32(3, 8, 128), f32(*mid), f32(*mid), f32(8, 128)],
        [scratch(*mid), scratch(*mid), scratch(*mid), scratch(8, 32, 128)],
        "down_1",
    )(wide1, tail1, xlo, xhi, ylo, yhi, k1, m1, f1, r01, side1, w)
    near = {k: shift(msg, "gz", k) for k in (1, -1, 2, -2, 3, -3)}
    r2z, wide2 = call(join_kernel, [f32(16, 8, 128), f32(8, 256)], [], "join")(
        msg, near[1], near[2], near[3], near[-3], near[-2], near[-1]
    )
    k2, k2u, m2, f2, k3, f3, r02, p02, side2 = call(
        weights_2_kernel,
        [
            bf16(768, 256), bf16(384, 128), bf16(768, 256), f32(8, 256), bf16(384, 128), f32(8, 128),
            bf16(512, 128), bf16(256, 128), f32(30, 32, 256),
        ],
        [], "weights_coarse",
    )(wide2)
    x1, x2, x3 = shift(r2z, "gx", 1), shift(r2z[:8], "gx", 2), shift(r2z, "gx", 3)
    r2x, low, high = call(edges_2_kernel, [f32(50, 8, 128), f32(18, 3, 128), f32(18, 3, 128)], [], "edges_2")(
        r2z, x1, x2, x3
    )
    ya, yb = shift(r2x, "gy", -1), shift(r2x, "gy", 1)
    yc, yd = shift(high, "gy", -2), shift(low, "gy", 2)
    lev2 = (30, 32, 256)
    sol, res, stat = call(
        up_kernel,
        [f32(32, 32, 128), f32(32, 32, 128), f32(1, 128)],
        [
            scratch(*lev2), scratch(*lev2), scratch(*lev2), scratch(12, 2, 40, 128),
            scratch(14, 32, 128), scratch(12, 16, 128), scratch(12, 16, 128), scratch(12, 16, 128),
            scratch(12, 32, 128), scratch(*mid), scratch(*mid), scratch(14, 32, 128),
            scratch(*big), scratch(*big), scratch(20, 2, 40, 128),
        ],
        "up", 24,
    )(
        r2x, ya, yb, yc, yd, k2, k2u, m2, f2, k3, f3, r02, p02, side2,
        k1u, f1, e1s, r1s, p01, side1, k0, m0, f0, e0s, r0s, p00, side0, stat0, stat1,
    )
    sol, res = call(
        store_kernel, [f32(32, 32, 128), f32(32, 32, 128)], [pltpu.SemaphoreType.DMA((2,))], "store", 4, (0, 1)
    )(sol, res)
    t = stat
    for axis, flips in (("gy", (1,)), ("gx", (1,)), ("gx", (3,)), ("gy", (2,)), ("gy", (6,)), ("gz", (1, 2, 3)), ("gz", (7,))):
        others = [swap(t, axis, f) for f in flips]
        t = t + others[0]
        if len(others) > 1:
            t = t + (others[1] + others[2])
    cells = jnp.array([NX * NY * NZ >> (3 * k) for k in (0, 1, 2, 0)], F32)
    return sol, res, jnp.sqrt(t[0, :4] / cells)


def solution(mesh):
    placed = (P("gx", "gy", "gz"), P(None, "gz"))
    return jax.shard_map(
        body,
        mesh=mesh,
        in_specs=placed,
        out_specs=(P("gx", "gy", "gz"), P("gx", "gy", "gz"), P()),
        check_vma=False,
    )
```

```python
import jax
import jax.numpy as jnp
from jax import lax
from jax.sharding import PartitionSpec as P
from jax.experimental import pallas as pl
from jax.experimental.pallas import tpu as pltpu

OFFSETS = (-4, -3, -2, -1, 1, 2, 3, 4)
RELAX = 0.45
NX, NY, NZ = 128, 256, 1024
F32, BF16 = jnp.float32, jnp.bfloat16
H0, H1, H2, H3 = 4, 5, 11, 4
S0, S1, S2, S3 = 1.0, 0.25, 0.0625, 0.015625
SLOT = 40
TAILS = {1: (0, 28), 2: (56, 20), 3: (96, 12), 4: (120, 4)}


def place_0(p):
    return jnp.where(p < 192, p, p - 256)


def place_1(p):
    lane = p & 127
    return jnp.where((lane < 96) == (p < 128), lane, lane - 128)


def place_2(p):
    lane = p & 127
    return jnp.where((lane < 80) == (p < 128), lane, lane - 128)


def place_3(p):
    return jnp.where(p < 64, p, p - 128)


def inside(z, iz, level, reach):
    count = 128 >> level
    glob = iz * count + z
    return (z >= -reach) & (z < count + reach) & (glob >= 0) & (glob < (NZ >> level))


def rows(shape, dim):
    return lax.broadcasted_iota(jnp.int32, shape, dim)


def halves(a):
    hi = a.astype(BF16)
    return hi, (a - hi.astype(F32)).astype(BF16)


def thrice(matrix):
    hi, lo = halves(matrix)
    return jnp.concatenate([hi, hi, lo], axis=0)


def times(field, matrix):
    shape = field.shape
    hi, lo = halves(field.reshape(shape[0] * shape[1], shape[2]))
    out = jnp.dot(jnp.concatenate([hi, lo, hi], axis=1), matrix, preferred_element_type=F32)
    return out.reshape(shape[0], shape[1], matrix.shape[1])


def times_exact(field, matrix):
    shape = field.shape
    hi, lo = halves(field.reshape(shape[0] * shape[1], shape[2]))
    out = jnp.dot(jnp.concatenate([hi, lo], axis=1), matrix, preferred_element_type=F32)
    return out.reshape(shape[0], shape[1], matrix.shape[1])


def exact(a, b):
    return jnp.dot(a, b, precision=lax.Precision.HIGHEST, preferred_element_type=F32)


def operators(w, place, iz, level, reach, stiffness):
    n = w.shape[1]
    zk = place(rows((n, n), 0))
    zn = place(rows((n, n), 1))
    both = inside(zk, iz, level, reach) & inside(zn, iz, level, reach)
    gap = jnp.where(both, zk - zn, 99)
    band = jnp.where(gap == 0, 1.0, 0.0)
    eye = jnp.where(rows((n, n), 0) == rows((n, n), 1), 1.0, 0.0)
    for j, offset in enumerate(OFFSETS):
        band = jnp.where(gap == offset, w[j : j + 1, :], band)
    gram = lax.dot_general(
        band, band, (((1,), (1,)), ((), ())), precision=lax.Precision.HIGHEST, preferred_element_type=F32
    )
    diag = jnp.sum(gram * eye, axis=0, keepdims=True) + 6.0 * stiffness
    line = inside(place(rows((1, n), 1)), iz, level, reach)
    factor = jnp.where(line, RELAX / diag, 0.0)
    op = gram + stiffness * (6.0 * eye - jnp.where((gap == 1) | (gap == -1), 1.0, 0.0))
    return band, op, eye - op * factor, factor


def restrict_matrix(place_f, n_f, place_c, n_c, iz, level, reach):
    zf = place_f(rows((n_f, n_c), 0))
    zc = place_c(rows((n_f, n_c), 1))
    gap = zf - 2 * zc
    near = jnp.where((gap == 0) | (gap == 1), 0.375, 0.0) + jnp.where((gap == -1) | (gap == 2), 0.125, 0.0)
    m = jnp.where(inside(zf, iz, level, reach), near, 0.0).astype(BF16)
    return jnp.concatenate([m, m], axis=0)


def prolong_matrix(place_c, n_c, place_f, n_f, iz, level, reach):
    zc = place_c(rows((n_c, n_f), 0))
    zf = place_f(rows((n_c, n_f), 1))
    gap = zf - 2 * zc
    near = jnp.where((gap == 0) | (gap == 1), 0.75, 0.0) + jnp.where((gap == -1) | (gap == 2), 0.25, 0.0)
    m = jnp.where(inside(zf, iz, level, reach), near, 0.0).astype(BF16)
    return jnp.concatenate([m, m], axis=0)


def plane_mask(shape, level, ix, iy, reach):
    x = ix * (32 >> level) + rows(shape, 0) - reach
    y = iy * (32 >> level) + rows(shape, 1) - reach
    ok = (x >= 0) & (x < (NX >> level)) & (y >= 0) & (y < (NY >> level))
    return jnp.where(ok, 1.0, 0.0)


def around(ref, a, b):
    mid = ref[a:b]
    count = mid.shape[1]
    return mid, (ref[a + 1 : b + 1] + ref[a - 1 : b - 1]) + (pltpu.roll(mid, 1, 1) + pltpu.roll(mid, count - 1, 1))


def chunks(a, b):
    mid = (a + b + 1) // 2
    return [(a, mid), (mid, b)]


def relax(src, dst, a, b, matrix, right, side, line=None):
    for p, q in chunks(a, b):
        mid, near = around(src, p, q)
        value = times(mid, matrix) + right(p, q) + side[p:q] * near
        dst[p:q] = value if line is None else value + mid * line


def pack_lanes(planes, height, width, count, to_left, to_right):
    lane = rows((height, 128), 1)
    for g in range(-(-len(planes) // 3)):
        left, right = None, None
        for i, value in enumerate(planes[3 * g : 3 * g + 3]):
            a = pltpu.roll(value, SLOT * i, 1) if i else value
            b = pltpu.roll(value, (SLOT * i + width - count) % 128, 1)
            left = a if i == 0 else jnp.where(lane < SLOT * i, left, a)
            right = b if i == 0 else jnp.where(lane < SLOT * i, right, b)
        to_left[g] = left
        to_right[g] = right


def prepare_kernel(data, weights, own, w, to_left, to_right, sems):
    copies = [
        pltpu.make_async_copy(data.at[pl.ds(8 * g, 8)], own.at[pl.ds(8 * g, 8)], sems.at[g]) for g in range(4)
    ]
    copies.append(pltpu.make_async_copy(weights, w, sems.at[4]))
    for copy in copies:
        copy.start()
    lane = rows((32, 128), 1)
    thin = [jnp.zeros((32, 128), F32)] * 2
    for g in range(8):
        if g % 2 == 0:
            copies[g // 2].wait()
        left, right = own[4 * g], None
        for i in range(4):
            p = 4 * g + i
            value = own[p]
            if i:
                left = jnp.where(lane < 32 * i, left, pltpu.roll(value, 32 * i, 1))
            b = pltpu.roll(value, 32 * i + 32, 1) if i < 3 else value
            right = b if i == 0 else jnp.where(lane < 32 * i, right, b)
            here = (lane >= 4 * p) & (lane < 4 * p + 4)
            thin[0] = jnp.where(here, pltpu.roll(value, (4 * p - 32) % 128, 1) if p != 8 else value, thin[0])
            thin[1] = jnp.where(here, pltpu.roll(value, (4 * p - 92) % 128, 1) if p != 23 else value, thin[1])
        to_left[32 * g : 32 * g + 32] = left
        to_right[32 * g : 32 * g + 32] = right
    to_left[256:288] = thin[0]
    to_right[256:288] = thin[1]
    copies[4].wait()
    to_left[288:296] = w[...]
    to_right[288:296] = w[...]


def turned(value, amount):
    return pltpu.roll(value, amount % 128, 1) if amount % 128 else value


def spread_0_kernel(own, from_right, from_left, tail, first, last):
    lane = rows((32, 128), 1)
    packed = [jnp.zeros((32, 128), F32)] * 2
    thin_right, thin_left = from_right[256:288], from_left[256:288]
    for p in range(32):
        g, i = divmod(p, 4)
        right = turned(from_right[32 * g : 32 * g + 32], -32 * i)
        left = turned(from_left[32 * g : 32 * g + 32], 96 - 32 * i)
        right = jnp.where(lane < 32, right, turned(thin_right, 32 - 4 * p))
        left = jnp.where(lane < 96, turned(thin_left, 92 - 4 * p), left)
        value = jnp.where(lane < 36, right, jnp.where(lane >= 92, left, 0.0))
        tail[p] = value
        for side, far in ((0, p + 1), (1, 32 - p)):
            if far <= H0:
                begin, reach = TAILS[far]
                moved = pltpu.roll(value, begin + reach, 1)
                packed[side] = jnp.where((lane >= begin) & (lane < begin + 2 * reach), moved, packed[side])
    first[:H0] = own[:H0]
    first[H0] = packed[0]
    last[:H0] = own[32 - H0 :]
    last[H0] = packed[1]


def edges_0_kernel(own, tail, xlo, xhi, low, high):
    lane = rows((4, 128), 1)

    def ends(ref, p):
        value = ref[p]
        return value[:H0], value[32 - H0 :]

    def tails(p):
        if H0 <= p < 32 + H0:
            return ends(tail, p - H0)
        source = xlo if p < H0 else xhi
        begin, reach = TAILS[H0 - p if p < H0 else p - 31 - H0]
        out = []
        for value in ends(source, H0):
            moved = pltpu.roll(value, (128 - begin - reach) % 128, 1)
            out.append(jnp.where((lane < reach) | (lane >= 128 - reach), moved, 0.0))
        return out

    kept = None
    for ref in (low, high):
        ref[60] = jnp.zeros((4, 128), F32)
    for p in range(40):
        if p < H0:
            a, b = ends(xlo, p)
        elif p < 32 + H0:
            a, b = ends(own, p - H0)
        else:
            a, b = ends(xhi, p - 32 - H0)
        low[p] = a
        high[p] = b
        moved = [pltpu.roll(v, 28 if p % 2 == 0 else 92, 1) for v in tails(p)]
        if p % 2 == 0:
            kept = moved
        else:
            low[40 + p // 2] = jnp.where(lane < 64, kept[0], moved[0])
            high[40 + p // 2] = jnp.where(lane < 64, kept[1], moved[1])


def gather_0_kernel(own, tail, xlo, xhi, field):
    ix = lax.axis_index("gx")
    lane = rows((32, 128), 1)
    for p in range(40):
        if H0 <= p < 32 + H0:
            field[p, 4:36, :128] = own[p - H0]
            field[p, 4:36, 128:] = tail[p - H0]
        else:
            source, q = (xlo, p) if p < H0 else (xhi, p - 32 - H0)
            begin, reach = TAILS[H0 - p if p < H0 else p - 31 - H0]
            xr = ix * 32 + p - H0
            ok = jnp.where((xr >= 0) & (xr < NX), 1.0, 0.0)
            moved = pltpu.roll(source[H0], (128 - begin - reach) % 128, 1)
            field[p, 4:36, :128] = source[q] * ok
            field[p, 4:36, 128:] = jnp.where((lane < reach) | (lane >= 128 - reach), moved, 0.0) * ok
        field[p, :4] = jnp.zeros((4, 256), F32)
        field[p, 36:] = jnp.zeros((4, 256), F32)


def weights_0_kernel(left, own, right, b0, k0, m0, f0, fold, grow, side):
    ix, iy, iz = lax.axis_index("gx"), lax.axis_index("gy"), lax.axis_index("gz")
    lane = rows((8, 128), 1)
    laid = jnp.concatenate([own[...], jnp.where(lane < 64, right[288:296], left[288:296])], axis=1)
    band, op, step, factor = operators(laid, place_0, iz, 0, 36, S0)
    eye = jnp.where(rows((256, 256), 0) == rows((256, 256), 1), 1.0, 0.0)
    lines = [factor]
    for out, matrix in ((k0, step), (m0, op), (b0, jnp.transpose(band))):
        own_part = matrix * eye
        out[...] = thrice(matrix - own_part)
        lines.append(jnp.sum(own_part, axis=0, keepdims=True))
    f0[...] = jnp.concatenate(lines + [jnp.zeros((4, 256), F32)], axis=0)
    fold[...] = restrict_matrix(place_0, 256, lambda q: q, 128, iz, 0, 36)
    grow[...] = prolong_matrix(place_1, 128, place_0, 256, iz, 0, 36)
    y = iy * 32 + rows((40, 256), 0) - H0
    column = jnp.where((y >= 0) & (y < NY), factor * S0, 0.0)
    for p in range(40):
        xr = ix * 32 + p - H0
        side[p] = column * jnp.where((xr >= 0) & (xr < NX), 1.0, 0.0)


def weights_1_kernel(left, own, right, k1, k1u, m1, f1, fold, grow, side):
    ix, iy, iz = lax.axis_index("gx"), lax.axis_index("gy"), lax.axis_index("gz")
    wide = jnp.concatenate([left[288:296], own[...], right[288:296]], axis=1)
    mean = jnp.where((rows((384, 256), 0) - 128) >> 1 == place_1(rows((384, 256), 1)), 0.5, 0.0)
    band, op, step, factor = operators(exact(wide, mean), place_1, iz, 1, 41, S1)
    k1[...] = thrice(step[:, :128])
    k1u[...] = thrice(step[:128, :128])
    m1[...] = thrice(op[:128, :128])
    f1[...] = jnp.broadcast_to(factor, (8, 256))
    fold[...] = restrict_matrix(place_1, 128, lambda q: q, 128, iz, 1, 32)
    grow[...] = prolong_matrix(place_2, 128, place_1, 128, iz, 1, 41)
    yrow = rows((32, 128), 0)
    y = iy * 16 + yrow - H1
    column = jnp.where((y >= 0) & (y < NY // 2) & (yrow < 26), factor[:, :128] * S1, 0.0)
    for p in range(26):
        xr = ix * 16 + p - H1
        side[p] = column * jnp.where((xr >= 0) & (xr < NX // 2), 1.0, 0.0)


def spread_1_kernel(own, from_right, from_left, main, rest, first, last):
    lane = rows((16, 128), 1)
    for p in range(16):
        group, i = divmod(p, 3)
        right = pltpu.roll(from_right[group], (64 - SLOT * i) % 128, 1)
        left = pltpu.roll(from_left[group], (91 - SLOT * i) % 128, 1)
        one = jnp.where(lane < 64, own[p], jnp.where(lane < 101, right, 0.0))
        two = jnp.where(lane >= 91, left, 0.0)
        main[p] = jnp.where(lane < 96, one, two)
        rest[p] = jnp.where(lane < 96, two, one)
    first[:H1] = main[:H1]
    first[H1] = rest[0]
    last[:H1] = main[16 - H1 :]
    last[H1] = rest[15]


def edges_1_kernel(main, rest, xlo, xhi, low, high):
    for p in range(26):
        if p < H1:
            value, tail = xlo[p], xlo[H1] if p == H1 - 1 else None
        elif p < 16 + H1:
            value, tail = main[p - H1], rest[p - H1]
        else:
            value, tail = xhi[p - 16 - H1], xhi[H1] if p == 16 + H1 else None
        low[p, :H1] = value[:H1]
        high[p, :H1] = value[16 - H1 :]
        none = jnp.zeros((8 - H1, 128), F32)
        low[p, H1:] = none
        high[p, H1:] = none
        if tail is not None:
            low[p, H1 : H1 + 1] = tail[0:1]
            high[p, H1 : H1 + 1] = tail[15:16]


def down_0_kernel(
    field, ylo, yhi, b0, k0, m0, f0, fold, side, r1, to_left, to_right, e_out, r_out, stat, d, e0, g, gx
):
    ix, iy, iz = lax.axis_index("gx"), lax.axis_index("gy"), lax.axis_index("gz")
    low_ok = jnp.where(iy > 0, 1.0, 0.0)
    high_ok = jnp.where(iy < 7, 1.0, 0.0)
    lane = rows((4, 128), 1)
    for p in range(40):
        xr = ix * 32 + p - H0
        ok = jnp.where((xr >= 0) & (xr < NX), 1.0, 0.0)
        d[p, 4:36] = field[p, 4:36]
        for edge, part, good in ((ylo, slice(0, 4), low_ok), (yhi, slice(36, 40), high_ok)):
            moved = pltpu.roll(edge[40 + p // 2], 100 if p % 2 == 0 else 36, 1)
            d[p, part, :128] = edge[p] * (ok * good)
            d[p, part, 128:] = jnp.where((lane < 28) | (lane >= 100), moved, 0.0) * (ok * good)
    factor, step_line, op_line, band_line = (f0[i : i + 1, :].reshape(1, 1, 256) for i in range(4))
    for p, q in chunks(0, 40):
        r = times(d[p:q], b0[...]) + d[p:q] * band_line
        r_out[p:q] = r
        e0[p:q] = r * factor
    relax(e0, e_out, 1, 39, k0[...], lambda p, q: e0[p:q], side, step_line)
    e_out[0] = jnp.zeros((40, 256), F32)
    e_out[39] = jnp.zeros((40, 256), F32)
    total = jnp.zeros((40, 128), F32)
    for p, q in chunks(3, 37):
        mid, near = around(e_out, p, q)
        value = (r_out[p:q] - mid * op_line) - times(mid, m0[...]) + S0 * near
        x = ix * 32 + rows(value.shape, 0) + (p - H0)
        y = iy * 32 + rows(value.shape, 1) - H0
        value = jnp.where((x >= 0) & (x < NX) & (y >= 0) & (y < NY), value, 0.0)
        g[p:q] = value
        own = value[max(p, 4) - p : min(q, 36) - p, :, :128]
        total = total + jnp.sum(own * own, axis=0)
    row = rows((40, 128), 0)
    stat[...] = jnp.full((8, 128), jnp.sum(jnp.where((row >= 4) & (row < 36), total, 0.0)), F32)
    for i in range(16):
        value = ((g[2 * i + 3] + g[2 * i + 6]) + 3.0 * (g[2 * i + 4] + g[2 * i + 5])) * 0.125
        gx[i, 0] = value[:, :128]
        gx[i, 1] = value[:, 128:]
    gy = [
        jnp.concatenate([gx[:, t, pl.ds(3 + a, 16, stride=2), :] for t in range(2)], axis=2) for a in range(4)
    ]
    gy = ((gy[0] + gy[3]) + 3.0 * (gy[1] + gy[2])) * 0.125
    out = times_exact(gy, fold[...])
    r1[...] = out
    pack_lanes([out[i] for i in range(16)], 16, 37, 64, to_left, to_right)


def down_1_kernel(wide, tail, xlo, xhi, ylo, yhi, k1, m1, f1, fold, side, w, msg, e_out, r_out, stat, e0, e0b, g, gx):
    ix, iy, iz = lax.axis_index("gx"), lax.axis_index("gy"), lax.axis_index("gz")
    lane = rows((32, 128), 1)
    yrow = rows((32, 128), 0)
    y = iy * 16 + yrow - H1
    inner = jnp.where((y >= 0) & (y < NY // 2) & (yrow < 26), 1.0, 0.0)
    for p in range(26):
        xr = ix * 16 + p - H1
        ok = inner * jnp.where((xr >= 0) & (xr < NX // 2), 1.0, 0.0)
        if p < H1:
            value, extra = xlo[p], xlo[H1] if p == H1 - 1 else jnp.zeros((16, 128), F32)
        elif p < 16 + H1:
            value, extra = wide[p - H1], tail[p - H1]
        else:
            value, extra = xhi[p - 16 - H1], xhi[H1] if p == 16 + H1 else jnp.zeros((16, 128), F32)
        main = jnp.concatenate([ylo[p, :H1], value, yhi[p, :H1], jnp.zeros((6, 128), F32)], axis=0) * ok
        rest = jnp.concatenate(
            [jnp.zeros((4, 128), F32), ylo[p, H1 : H1 + 1], extra, yhi[p, H1 : H1 + 1], jnp.zeros((10, 128), F32)],
            axis=0,
        ) * ok
        r_out[p] = main
        e0[p] = main * f1[0:1, :128]
        e0b[p] = rest * f1[0:1, 128:]
    for p, q in chunks(1, 25):
        mid, near = around(e0, p, q)
        both = jnp.concatenate([mid, e0b[p:q]], axis=2)
        e_out[p:q] = times(both, k1[...]) + mid + side[p:q] * near
    e_out[0] = jnp.zeros((32, 128), F32)
    e_out[25] = jnp.zeros((32, 128), F32)
    total = jnp.zeros((32, 128), F32)
    for p, q in chunks(4, 22):
        mid, near = around(e_out, p, q)
        value = r_out[p:q] - times(mid, m1[...]) + S1 * near
        x = ix * 16 + rows(value.shape, 0) + (p - H1)
        y = iy * 16 + rows(value.shape, 1) - H1
        value = jnp.where((x >= 0) & (x < NX // 2) & (y >= 0) & (y < NY // 2), value, 0.0)
        g[p:q] = value
        own = value[max(p, 5) - p : min(q, 21) - p]
        total = total + jnp.sum(own * own, axis=0)
    row = rows((32, 128), 0)
    keep = (row >= 5) & (row < 21) & (lane < 64)
    stat[...] = jnp.full((8, 128), jnp.sum(jnp.where(keep, total, 0.0)), F32)
    for i in range(8):
        gx[i] = ((g[2 * i + 4] + g[2 * i + 7]) + 3.0 * (g[2 * i + 5] + g[2 * i + 6])) * 0.125
    gy = [gx[:, pl.ds(4 + a, 8, stride=2), :] for a in range(4)]
    gy = ((gy[0] + gy[3]) + 3.0 * (gy[1] + gy[2])) * 0.125
    out = times_exact(gy, fold[...])[:, :, :32]
    for k in range(2):
        msg[k] = jnp.concatenate([out[4 * k + i] for i in range(4)], axis=1)
    mean = jnp.where(rows((128, 128), 0) >> 2 == rows((128, 128), 1), 0.25, 0.0)
    msg[2] = exact(w[...], mean)


def join_kernel(own, r1, r2, r3, l3, l2, l1, both, w):
    lane = rows((8, 128), 1)
    blocks = (own, r1, r2, r3), (None, l3, l2, l1)
    for p in range(9):
        k, i = divmod(p, 4)
        part = slice(32 * i, 32 * i + 32)
        first, second = (
            jnp.concatenate([jnp.zeros((8, 32), F32) if b is None else b[k, :, part] for b in group], axis=1)
            for group in blocks
        )
        main, rest = jnp.where(lane < 80, first, second), jnp.where(lane < 80, second, first)
        if p < 8:
            both[p] = main
            both[8 + p] = rest
        else:
            w[:, :128] = main
            w[:, 128:] = rest


def edges_2_kernel(own, x1, x2, x3, near, low, high):
    near[:3] = x2[5:]
    near[3:11] = x3[:8]
    near[11:19] = own[:8]
    near[19:27] = x1[:8]
    near[27:30] = x2[:3]
    near[30:36] = x3[10:]
    near[36:44] = own[8:]
    near[44:50] = x1[8:14]
    for ref in (low, high):
        ref[18] = jnp.zeros((3, 128), F32)
    for i in range(18):
        value = near[i + 6]
        low[i] = value[:3]
        high[i] = value[5:]


def weights_2_kernel(w2, k2, k2u, m2, f2, k3, f3, fold, grow, side):
    ix, iy, iz = lax.axis_index("gx"), lax.axis_index("gy"), lax.axis_index("gz")
    band, op, step, factor = operators(w2[...], place_2, iz, 2, 69, S2)
    k2[...] = thrice(step)
    k2u[...] = thrice(step[:128, :128])
    m2[...] = thrice(op)
    f2[...] = jnp.broadcast_to(factor, (8, 256))
    fold[...] = restrict_matrix(place_2, 256, place_3, 128, iz, 2, 65)
    grow[...] = prolong_matrix(place_3, 128, place_2, 128, iz, 2, 69)
    yrow = rows((32, 256), 0)
    y = iy * 8 + yrow - H2
    column = jnp.where((y >= 0) & (y < NY // 4) & (yrow < 30), factor * S2, 0.0)
    for p in range(30):
        xr = ix * 8 + p - H2
        side[p] = column * jnp.where((xr >= 0) & (xr < NX // 4), 1.0, 0.0)
    mean = jnp.where(place_2(rows((256, 128), 0)) >> 1 == place_3(rows((256, 128), 1)), 0.5, 0.0)
    band, op, step, factor = operators(exact(w2[...], mean), place_3, iz, 3, 28, S3)
    k3[...] = thrice(step)
    f3[...] = jnp.broadcast_to(factor, (8, 128))


def up_kernel(
    r2x, ya, yb, yc, yd, k2, k2u, m2, f2, k3, f3, fold2, grow2, side2,
    k1, f1, e1s, r1s, grow1, side1, k0, m0, f0, e0s, r0s, grow0, side0, stat0, stat1,
    sol, res, stat,
    ra, ea, eb, gx2, r3, e3, side3, c3, cy2, ua, ub, cy1, va, vb, cy0,
):
    ix, iy, iz = lax.axis_index("gx"), lax.axis_index("gy"), lax.axis_index("gz")
    lane = rows((32, 128), 1)
    yrow = rows((32, 128), 0)
    for p in range(30):
        xr = ix * 8 + p - H2
        y = iy * 8 + yrow - H2
        ok = jnp.where(
            (y >= 0) & (y < NY // 4) & (yrow < 30), jnp.where((xr >= 0) & (xr < NX // 4), 1.0, 0.0), 0.0
        )
        three, two = jnp.zeros((3, 128), F32), jnp.zeros((2, 128), F32)
        far = 6 <= p < 24
        main = jnp.concatenate(
            [yc[p - 6] if far else three, ya[p], r2x[p], yb[p], yd[p - 6] if far else three, two], axis=0
        ) * ok
        rest = jnp.zeros((32, 128), F32)
        if 5 <= p < 25:
            rest = jnp.concatenate([three, ya[p + 25], r2x[p + 25], yb[p + 25], three, two], axis=0) * ok
        ra[p, :, :128] = main
        ra[p, :, 128:] = rest
        ea[p, :, :128] = main * f2[0:1, :128]
        ea[p, :, 128:] = rest * f2[0:1, 128:]
    relax(ea, eb, 1, 29, k2[...], lambda p, q: ea[p:q], side2)
    total = jnp.zeros((32, 128), F32)
    for p, q in chunks(2, 28):
        mid, near = around(eb, p, q)
        value = ra[p:q] - times(mid, m2[...]) + S2 * near
        x = ix * 8 + rows(value.shape, 0) + (p - H2)
        y = iy * 8 + rows(value.shape, 1) - H2
        value = jnp.where((x >= 0) & (x < NX // 4) & (y >= 0) & (y < NY // 4), value, 0.0)
        ea[p:q] = value
        own = value[max(p, 11) - p : min(q, 19) - p, :, :128]
        total = total + jnp.sum(own * own, axis=0)
    keep = (yrow >= 11) & (yrow < 19) & (lane < 32)
    sum2 = jnp.sum(jnp.where(keep, total, 0.0))
    for i in range(12):
        value = ((ea[2 * i + 2] + ea[2 * i + 5]) + 3.0 * (ea[2 * i + 3] + ea[2 * i + 4])) * 0.125
        gx2[i, 0, :32] = value[:, :128]
        gx2[i, 1, :32] = value[:, 128:]
        gx2[i, 0, 32:] = jnp.zeros((8, 128), F32)
        gx2[i, 1, 32:] = jnp.zeros((8, 128), F32)
    gy = [
        jnp.concatenate([gx2[:, t, pl.ds(2 + a, 16, stride=2), :] for t in range(2)], axis=2) for a in range(4)
    ]
    gy = ((gy[0] + gy[3]) + 3.0 * (gy[1] + gy[2])) * 0.125
    mask = plane_mask((12, 16, 128), 3, ix, iy, H3)
    right3 = times_exact(gy, fold2[...]) * mask
    factor3 = f3[0:1, :].reshape(1, 1, 128)
    e3[...] = right3 * factor3
    side3[...] = mask * (factor3 * S3)
    c3[...] = jnp.zeros((12, 16, 128), F32)
    relax(e3, c3, 1, 11, k3[...], lambda p, q: e3[p:q], side3)
    cz = times_exact(c3[...], grow2[...])
    below, above = pltpu.roll(cz, 1, 1), pltpu.roll(cz, 15, 1)
    cy2[...] = jnp.zeros((12, 40, 128), F32)
    cy2[:, pl.ds(3, 12, stride=2), :] = (0.75 * cz + 0.25 * below)[:, :12]
    cy2[:, pl.ds(4, 12, stride=2), :] = (0.75 * cz + 0.25 * above)[:, :12]
    fr2 = f2[0:1, :128].reshape(1, 1, 128)
    for xf in range(6, 24):
        f = xf - H2
        j = f // 2 + 4
        other = j - 1 if f % 2 == 0 else j + 1
        xr = ix * 8 + f
        y = iy * 8 + yrow - H2
        ok = jnp.where((y >= 0) & (y < NY // 4), jnp.where((xr >= 0) & (xr < NX // 4), 1.0, 0.0), 0.0)
        ea[xf, :, :128] = eb[xf, :, :128] + ok * (0.75 * cy2[j, :32] + 0.25 * cy2[other, :32])

    def relax_2(src, dst, a, b):
        for p, q in chunks(a, b):
            mid = src[p:q, :, :128]
            near = (src[p + 1 : q + 1, :, :128] + src[p - 1 : q - 1, :, :128]) + (
                pltpu.roll(mid, 1, 1) + pltpu.roll(mid, 31, 1)
            )
            dst[p:q, :, :128] = times(mid, k2u[...]) + fr2 * ra[p:q, :, :128] + side2[p:q, :, :128] * near

    relax_2(ea, eb, 7, 23)
    relax_2(eb, ea, 8, 22)
    for p in range(14):
        r3[p] = ea[8 + p, :, :128]
    r3[...] = times_exact(r3[...], grow1[...])
    cy1[...] = jnp.zeros((14, 40, 128), F32)
    cy1[:, pl.ds(1, 12, stride=2), :] = 0.75 * r3[:, 9:21, :] + 0.25 * r3[:, 8:20, :]
    cy1[:, pl.ds(2, 12, stride=2), :] = 0.75 * r3[:, 9:21, :] + 0.25 * r3[:, 10:22, :]
    fr1 = f1[0:1, :128].reshape(1, 1, 128)
    for xf in range(1, 25):
        f = xf - H1
        xr = ix * 16 + f
        y = iy * 16 + yrow - H1
        ok = jnp.where((y >= 0) & (y < NY // 2), jnp.where((xr >= 0) & (xr < NX // 2), 1.0, 0.0), 0.0)
        j = f // 2 + 3
        other = j - 1 if f % 2 == 0 else j + 1
        ua[xf] = e1s[xf] + ok * (0.75 * cy1[j, :32] + 0.25 * cy1[other, :32])
    relax(ua, ub, 2, 24, k1[...], lambda p, q: fr1 * r1s[p:q], side1)
    relax(ub, ua, 3, 23, k1[...], lambda p, q: fr1 * r1s[p:q], side1)
    for p, q in chunks(0, 20):
        cz = times_exact(ua[3 + p : 3 + q], grow0[...])
        for t in range(2):
            part = cz[:, :, 128 * t : 128 * t + 128]
            cy0[p:q, t, pl.ds(0, 20, stride=2), :] = 0.75 * part[:, 3:23] + 0.25 * part[:, 2:22]
            cy0[p:q, t, pl.ds(1, 20, stride=2), :] = 0.75 * part[:, 3:23] + 0.25 * part[:, 4:24]
    fr0, step_line, op_line = (f0[i : i + 1, :].reshape(1, 1, 256) for i in range(3))
    for xf in range(1, 39):
        f = xf - H0
        xr = ix * 32 + f
        y = iy * 32 + rows((40, 128), 0) - H0
        ok = jnp.where((y >= 0) & (y < NY), jnp.where((xr >= 0) & (xr < NX), 1.0, 0.0), 0.0)
        for t in range(2):
            part = slice(128 * t, 128 * t + 128)
            j = f // 2 + 2
            other = j - 1 if f % 2 == 0 else j + 1
            va[xf, :, part] = e0s[xf, :, part] + ok * (0.75 * cy0[j, t, :40] + 0.25 * cy0[other, t, :40])
    relax(va, vb, 2, 38, k0[...], lambda p, q: fr0 * r0s[p:q], side0, step_line)
    relax(vb, va, 3, 37, k0[...], lambda p, q: fr0 * r0s[p:q], side0, step_line)
    total = jnp.zeros((32, 128), F32)
    last = m0[:, :128]
    for p, q in chunks(4, 36):
        mid = va[p:q]
        flat = va[p:q, :, :128]
        near = (va[p + 1 : q + 1, :, :128] + va[p - 1 : q - 1, :, :128]) + (
            pltpu.roll(flat, 1, 1) + pltpu.roll(flat, 39, 1)
        )
        value = ((r0s[p:q, :, :128] - flat * op_line[:, :, :128]) - times(mid, last) + S0 * near)[:, 4:36]
        part = slice(p - 4, q - 4)
        res[part] = value
        sol[part] = va[p:q, 4:36, :128]
        total = total + jnp.sum(value * value, axis=0)
    sum3 = jnp.sum(total)
    tile = rows((8, 128), 1)
    stat[...] = jnp.where(
        tile == 0, stat0[...], jnp.where(tile == 1, stat1[...], jnp.where(tile == 2, sum2, jnp.where(tile == 3, sum3, 0.0)))
    )


def store_kernel(a, b, a_out, b_out, sems):
    sends = [pltpu.make_async_copy(x, y, sems.at[i]) for i, (x, y) in enumerate(((a, a_out), (b, b_out)))]
    for send in sends:
        send.start()
    for send in sends:
        send.wait()


def shift(x, axis, k):
    n = lax.axis_size(axis)
    return lax.ppermute(x, axis, [((i + k) % n, i) for i in range(n)])


def swap(x, axis, flip):
    return lax.ppermute(x, axis, [(i ^ flip, i) for i in range(lax.axis_size(axis))])


def f32(*shape):
    return pltpu.VMEM(shape, F32)


def bf16(*shape):
    return pltpu.VMEM(shape, BF16)


def scratch(*shape):
    return pltpu.VMEM(shape, F32)


def call(kernel, outs, scratches, name, limit=16, away=(), home=()):
    def run(*operands):
        operands = [
            pltpu.with_memory_space_constraint(x, pltpu.HBM if i in home else pltpu.VMEM)
            for i, x in enumerate(operands)
        ]
        return pl.pallas_call(
            kernel,
            out_shape=[jax.ShapeDtypeStruct(o.shape, F32) if i in away else o for i, o in enumerate(outs)],
            in_specs=[pl.BlockSpec(memory_space=pltpu.HBM if i in home else pltpu.VMEM) for i in range(len(operands))],
            out_specs=[pl.BlockSpec(memory_space=pl.ANY if i in away else pltpu.VMEM) for i in range(len(outs))],
            scratch_shapes=scratches,
            compiler_params=pltpu.CompilerParams(vmem_limit_bytes=limit * 2**20),
            name=name,
        )(*operands)

    return run


def body(data, weights):
    own, w, to_left, to_right = call(
        prepare_kernel,
        [f32(32, 32, 128), f32(8, 128), f32(296, 128), f32(296, 128)],
        [pltpu.SemaphoreType.DMA((5,))], "prepare", home=(0, 1),
    )(data, weights)
    from_right, from_left = shift(to_left, "gz", 1), shift(to_right, "gz", -1)
    tail, first, last = call(
        spread_0_kernel, [f32(32, 32, 128), f32(5, 32, 128), f32(5, 32, 128)], [], "spread_0"
    )(own, from_right, from_left)
    xlo, xhi = shift(last, "gx", -1), shift(first, "gx", 1)
    low, high = call(edges_0_kernel, [f32(62, 4, 128), f32(62, 4, 128)], [], "edges_0")(own, tail, xlo, xhi)
    ylo, yhi = shift(high, "gy", -1), shift(low, "gy", 1)
    (field,) = call(gather_0_kernel, [f32(40, 40, 256)], [], "gather_0")(own, tail, xlo, xhi)
    b0, k0, m0, f0, r00, p00, side0 = call(
        weights_0_kernel,
        [
            bf16(768, 256), bf16(768, 256), bf16(768, 256), f32(8, 256), bf16(512, 128), bf16(256, 256),
            f32(40, 40, 256),
        ],
        [], "weights_0",
    )(from_left, w, from_right)
    k1, k1u, m1, f1, r01, p01, side1 = call(
        weights_1_kernel,
        [
            bf16(768, 128), bf16(384, 128), bf16(384, 128), f32(8, 256), bf16(256, 128), bf16(256, 128),
            f32(26, 32, 128),
        ],
        [], "weights_1",
    )(from_left, w, from_right)
    big = (40, 40, 256)
    r1, to_left, to_right, e0s, r0s, stat0 = call(
        down_0_kernel,
        [f32(16, 16, 128), f32(6, 16, 128), f32(6, 16, 128), f32(*big), f32(*big), f32(8, 128)],
        [scratch(*big), scratch(*big), scratch(*big), scratch(16, 2, 40, 128)],
        "down_0",
    )(field, ylo, yhi, b0, k0, m0, f0, r00, side0)
    from_right, from_left = shift(to_left, "gz", 1), shift(to_right, "gz", -1)
    wide1, tail1, first, last = call(
        spread_1_kernel, [f32(16, 16, 128), f32(16, 16, 128), f32(6, 16, 128), f32(6, 16, 128)], [], "spread_1"
    )(r1, from_right, from_left)
    xlo, xhi = shift(last, "gx", -1), shift(first, "gx", 1)
    low, high = call(edges_1_kernel, [f32(26, 8, 128), f32(26, 8, 128)], [], "edges_1")(wide1, tail1, xlo, xhi)
    ylo, yhi = shift(high, "gy", -1), shift(low, "gy", 1)
    mid = (26, 32, 128)
    msg, e1s, r1s, stat1 = call(
        down_1_kernel,
        [f32(3, 8, 128), f32(*mid), f32(*mid), f32(8, 128)],
        [scratch(*mid), scratch(*mid), scratch(*mid), scratch(8, 32, 128)],
        "down_1",
    )(wide1, tail1, xlo, xhi, ylo, yhi, k1, m1, f1, r01, side1, w)
    near = {k: shift(msg, "gz", k) for k in (1, -1, 2, -2, 3, -3)}
    r2z, wide2 = call(join_kernel, [f32(16, 8, 128), f32(8, 256)], [], "join")(
        msg, near[1], near[2], near[3], near[-3], near[-2], near[-1]
    )
    k2, k2u, m2, f2, k3, f3, r02, p02, side2 = call(
        weights_2_kernel,
        [
            bf16(768, 256), bf16(384, 128), bf16(768, 256), f32(8, 256), bf16(384, 128), f32(8, 128),
            bf16(512, 128), bf16(256, 128), f32(30, 32, 256),
        ],
        [], "weights_coarse",
    )(wide2)
    x1, x2, x3 = shift(r2z, "gx", 1), shift(r2z[:8], "gx", 2), shift(r2z, "gx", 3)
    r2x, low, high = call(edges_2_kernel, [f32(50, 8, 128), f32(20, 3, 128), f32(20, 3, 128)], [], "edges_2")(
        r2z, x1, x2, x3
    )
    ya, yb = shift(r2x, "gy", -1), shift(r2x, "gy", 1)
    yc, yd = shift(high, "gy", -2), shift(low, "gy", 2)
    lev2 = (30, 32, 256)
    sol, res, stat = call(
        up_kernel,
        [f32(32, 32, 128), f32(32, 32, 128), f32(8, 128)],
        [
            scratch(*lev2), scratch(*lev2), scratch(*lev2), scratch(12, 2, 40, 128),
            scratch(14, 32, 128), scratch(12, 16, 128), scratch(12, 16, 128), scratch(12, 16, 128),
            scratch(12, 40, 128), scratch(*mid), scratch(*mid), scratch(14, 40, 128),
            scratch(*big), scratch(*big), scratch(20, 2, 48, 128),
        ],
        "up", 24,
    )(
        r2x, ya, yb, yc, yd, k2, k2u, m2, f2, k3, f3, r02, p02, side2,
        k1u, f1, e1s, r1s, p01, side1, k0, m0, f0, e0s, r0s, p00, side0, stat0, stat1,
    )
    sol, res = call(
        store_kernel, [f32(32, 32, 128), f32(32, 32, 128)], [pltpu.SemaphoreType.DMA((2,))], "store", 4, (0, 1)
    )(sol, res)
    t = stat
    for axis, flips in (("gy", (1,)), ("gx", (1, 2, 3)), ("gy", (2, 4, 6)), ("gz", (1, 2, 3)), ("gz", (7,))):
        others = [swap(t, axis, f) for f in flips]
        t = t + others[0]
        if len(others) > 1:
            t = t + (others[1] + others[2])
    cells = jnp.array([NX * NY * NZ >> (3 * k) for k in (0, 1, 2, 0)], F32)
    return sol, res, jnp.sqrt(t[0, :4] / cells)


def solution(mesh):
    placed = (P("gx", "gy", "gz"), P(None, "gz"))
    return jax.shard_map(
        body,
        mesh=mesh,
        in_specs=placed,
        out_specs=(P("gx", "gy", "gz"), P("gx", "gy", "gz"), P()),
        check_vma=False,
    )
```
